32 devices in a mesh: xs: 4 (over y, x), ax: 8 (over z, core).
Axes of the slice: x: 2, y: 2, z: 4, core: 2. Of those that a mesh axis runs over, the one named last changes fastest.
Arguments:
- concentration: float32 [256, 128, 384], P('ax', 'xs'), may hold values from -4 to 4
- tissue_mask: int32 [256, 128, 384], P('ax', 'xs'), may hold values from 0 to 1
- wall_layer: int32 [256, 128, 384], P('ax', 'xs'), may hold values from 0 to 3, as said below
- stiffness: float32 [256, 128, 384], P('ax', 'xs'), may hold values from 1 to 2
- production: float32 [256, 128, 384], P('ax', 'xs'), may hold values from -3 to 3
- layer_diffusivity: float32 [4], replicated, may hold values from 1 to 2
- uptake_rate: float32 [4], replicated, may hold values from 0.1 to 0.5
Outputs:
- concentration_out: float32 [256, 128, 384], P('ax', 'xs')
The draws below stay inside these ranges and needn't reach their ends.
Inputs may be any that keep to these rules, and one draw needn't show every extreme that they name: `wall_layer`: indexes the tables of layer coefficients.
All inputs are finite; a program needn't handle non-finite values.
Results may differ from the reference program's by a relative error of at most 0.0003.
Values sent between devices are 32-bit elements; how exact they have to be, the bound alone decides.
A program may use at most 128 MiB of HBM per device.

```python
import math
import jax
import jax.numpy as jnp
from jax import lax

NY = 384
STEPS = 2
LAYERS = 4
NX = 128
NZ = 256
RZ = 3072


def wall_geometry(key):
    base_key = jax.random.fold_in(key, 11)
    subkeys = jax.random.split(base_key, 3)
    centre_x = NX // 2 + jax.random.randint(subkeys[0], (), -(NX // 8), NX // 8 + 1)
    centre_y = NY // 2 + jax.random.randint(subkeys[1], (), -(NY // 8), NY // 8 + 1)
    bulge_start = jax.random.randint(subkeys[2], (), 0, NZ - NZ // 4 + 1)
    lumen_radius = NX // 4
    bulge_size = max(NX // 16, 1)
    layer_width = max(NX // 16, 1)
    axial = jnp.arange(NZ, dtype=jnp.int32)[:, None, None]
    across = jnp.arange(NX, dtype=jnp.int32)[None, :, None]
    along_y = jnp.arange(NY, dtype=jnp.int32)[None, None, :]
    inside = ((axial >= bulge_start) & (axial < bulge_start + NZ // 4)).astype(jnp.int32)
    radius = lumen_radius + bulge_size * inside
    radial_sq = (across - centre_x) * (across - centre_x) + (along_y - centre_y) * (along_y - centre_y)
    return (radius, radial_sq, layer_width)


def draw_tissue_mask(key, part):
    radius, radial_sq, layer_width = wall_geometry(key)
    return (radial_sq >= radius * radius).astype(jnp.int32)


def draw_wall_layer(key, part):
    radius, radial_sq, layer_width = wall_geometry(key)
    labels = jnp.zeros(radial_sq.shape, jnp.int32)
    for band_index in range(1, 4):
        edge = radius + band_index * layer_width
        labels = labels + (radial_sq >= edge * edge).astype(jnp.int32)
    return labels


def draw_concentration(key, part):
    base_key = jax.random.fold_in(key, 23)
    return jnp.clip(jax.random.normal(base_key, (NZ, NX, NY), jnp.float32), -4.0, 4.0)


def block_scale(rng, extent, cuts, low, largest):
    factor_of = 1.0
    for axis_at, blocks in cuts:
        heights = jax.random.uniform(jax.random.fold_in(jax.random.fold_in(rng, 6), axis_at), (blocks,), jnp.float32, low / len(cuts), largest / len(cuts))
        factor_of = factor_of * jnp.repeat(jnp.exp(heights), extent[axis_at] // blocks).reshape((-1,) + (1,) * (len(extent) - 1 - axis_at))
    return factor_of


def centred(key, extent, width, limit, cuts=(), held_as=jnp.bfloat16):
    array = jax.random.normal(key, extent, jnp.float32) * width
    if len(cuts) > 0:
        array = block_scale(key, extent, cuts, -0.22, 0.18) * array
    return jnp.clip(array, min=-limit, max=limit).astype(held_as)


def setup_inputs(seed: int = 0) -> dict:
    keys = jax.random.split(jax.random.key(seed), 8)
    return {
        "concentration": draw_concentration(jax.random.fold_in(keys[7], 71), 0),
        "tissue_mask": draw_tissue_mask(jax.random.fold_in(keys[7], 71), 0),
        "wall_layer": draw_wall_layer(jax.random.fold_in(keys[7], 71), 0),
        "stiffness": jnp.clip(jnp.exp(math.log(2.0) - 0.6931472 * jax.random.uniform(keys[3], (NZ, NX, NY), jnp.float32) ** block_scale(keys[3], (NZ, NX, NY), ((0, 8), (1, 4)), -0.2, 0.2)), 1.0, 2.0),
        "production": centred(keys[4], (NZ, NX, NY), 0.5, 3.0, ((0, 8), (1, 4)), jnp.float32),
        "layer_diffusivity": jnp.clip(jnp.exp(jax.random.uniform(keys[5], (LAYERS,), jnp.float32, math.log(1.0), math.log(2.0))), 1.0, 2.0),
        "uptake_rate": jnp.clip(jnp.exp(jax.random.uniform(keys[6], (LAYERS,), jnp.float32, math.log(0.1), math.log(0.5))), 0.1, 0.5),
    }


SECTION_RATE = 0.05

def table_lookup(labels, coeffs):
    summed = jnp.zeros(labels.shape, jnp.float32)
    for layer_index in range(coeffs.shape[0]):
        summed = summed + jnp.where(labels == layer_index, coeffs[layer_index], 0.0)
    return summed

def lower_neighbour(values, axis_id):
    zero_plane = jnp.zeros_like(lax.slice_in_dim(values, 0, 1, axis=axis_id))
    kept = lax.slice_in_dim(values, 0, values.shape[axis_id] - 1, axis=axis_id)
    return jnp.concatenate([zero_plane, kept], axis=axis_id)

def upper_neighbour(values, axis_id):
    zero_plane = jnp.zeros_like(lax.slice_in_dim(values, 0, 1, axis=axis_id))
    kept = lax.slice_in_dim(values, 1, values.shape[axis_id], axis=axis_id)
    return jnp.concatenate([kept, zero_plane], axis=axis_id)

def axial_solve(lower_band, diagonal, upper_band, rhs_vals):

    def forward(carried, row_data):
        prev_ratio, prev_value = carried
        low_coef, diag_coef, high_coef, right_side = row_data
        pivot = diag_coef - low_coef * prev_ratio
        new_ratio = high_coef / pivot
        new_value = (right_side - low_coef * prev_value) / pivot
        return ((new_ratio, new_value), (new_ratio, new_value))
    zero_plane = jnp.zeros(rhs_vals.shape[1:], jnp.float32)
    _, (ratios, values) = lax.scan(forward, (zero_plane, zero_plane), (lower_band, diagonal, upper_band, rhs_vals))

    def backward(next_value, row_data):
        ratio_row, value_row = row_data
        solved_row = value_row - ratio_row * next_value
        return (solved_row, solved_row)
    _, solved = lax.scan(backward, zero_plane, (ratios, values), reverse=True)
    return solved

def reference(concentration, tissue_mask, wall_layer, stiffness, production, layer_diffusivity, uptake_rate):
    tissue_weight = tissue_mask.astype(jnp.float32)
    diffusivity = tissue_weight * table_lookup(wall_layer, layer_diffusivity) * stiffness
    uptake_cell = tissue_weight * table_lookup(wall_layer, uptake_rate)
    source_cell = tissue_weight * production
    weights = []
    for axis_id in range(3):
        weights.append((jnp.sqrt(diffusivity * lower_neighbour(diffusivity, axis_id)), jnp.sqrt(diffusivity * upper_neighbour(diffusivity, axis_id))))
    lower_band = -RZ * weights[0][0]
    upper_band = -RZ * weights[0][1]
    diagonal = 1.0 + RZ * (weights[0][0] + weights[0][1])
    state_now = concentration
    for step_index in range(STEPS):
        net_flux = jnp.zeros_like(state_now)
        for axis_id in (1, 2):
            net_flux = net_flux + weights[axis_id][0] * (lower_neighbour(state_now, axis_id) - state_now)
            net_flux = net_flux + weights[axis_id][1] * (upper_neighbour(state_now, axis_id) - state_now)
        explicit = state_now + SECTION_RATE * net_flux
        solved = axial_solve(lower_band, diagonal, upper_band, explicit)
        state_now = solved + (source_cell - uptake_cell * solved)
    return state_now
```

```python
import functools

import jax
import jax.numpy as jnp
from jax import lax
from jax.experimental import pallas as pl
from jax.experimental.pallas import tpu as pltpu
from jax.sharding import PartitionSpec as P

STEPS = 2
RZ = 3072
SECTION_RATE = 0.05
MESH = pl.DeviceIdType.MESH


def lookup(labels, table_ref):
    summed = jnp.zeros(labels.shape, jnp.float32)
    for index in range(table_ref.shape[0]):
        summed = jnp.where(labels == index, table_ref[index], summed)
    return summed


def kernel(
    n_ax, n_xs,
    conc_hbm, mask_hbm, layer_hbm, stiff_hbm, prod_hbm, diff_hbm, upt_hbm,
    out_ref,
    diff_tab, upt_tab,
    mask, layer, stiff, source, state, root, ratio, recip, prodr, part, plane, side, uptake,
    edge, halo, shut, beyond, scales, middle, dev_c, pair_c, chip_c, links, solve_c,
    dev_v, pair_v, raw_v, fold_v, fold_out, flow, back_out,
    in_sem, xs_send, xs_recv, ax_send, ax_recv,
    pc_send, pc_recv, pv_send, pv_recv, bk_send, bk_recv, cc_send, cc_recv, cv_send, cv_recv,
):
    m, slab, cols = conc_hbm.shape
    chips = n_ax // 2
    half = slab // 2
    q = slab // 4
    f32 = jnp.float32
    me = lax.axis_index("ax")
    mx = lax.axis_index("xs")
    chip = lax.div(me, 2)
    core = lax.rem(me, 2)
    low = core == 0
    mate = {"ax": me + 1 - 2 * core}

    inside, ends = ((q, half + q),), ((0, q), (half + q, slab))
    spans = (inside, ends)
    own = (jnp.where(low, q, half), jnp.where(low, 0, half + q))
    other = (jnp.where(low, half, q), jnp.where(low, half + q, 0))

    def lines(starts, group):
        return pl.ds(pl.multiple_of(starts[group], 8), q)

    def kept(group):
        return slice(group * q, (group + 1) * q)

    def kept_ds(group):
        return pl.ds(group * q, q)

    def local(src, dst, at):
        return pltpu.make_async_copy(src, dst, in_sem.at[at])

    arrays = [(mask_hbm, mask), (layer_hbm, layer), (stiff_hbm, stiff)]
    tables = [local(diff_hbm, diff_tab, 0), local(upt_hbm, upt_tab, 1)]
    outer_loads = [
        local(src.at[z], dst.at[z], 2 + 2 * at + k)
        for at, (src, dst) in enumerate(arrays) for k, z in enumerate((0, m - 1))
    ]
    inner = pl.ds(1, m - 2)
    inner_loads = [local(src.at[inner], dst.at[inner], 8 + at) for at, (src, dst) in enumerate(arrays)]
    conc_load = local(conc_hbm, state, 11)
    prod_load = local(prod_hbm, source, 12)
    for load in tables + outer_loads + inner_loads + [conc_load, prod_load]:
        load.start()

    sides = (
        (mx > 0, {"xs": mx - 1}),
        (mx < n_xs - 1, {"xs": mx + 1}),
        (me > 0, {"ax": me - 1}),
        (me < n_ax - 1, {"ax": me + 1}),
    )
    far = []
    for reach in range(chips - 1, 0, -1):
        far.append((chip + reach < chips, chip + reach))
        far.append((chip - reach >= 0, chip - reach))
    greeted = list(sides) + [(there, {"ax": 2 * at + core}) for there, at in far]
    barrier = pltpu.get_barrier_semaphore()
    for there, peer in greeted:
        @pl.when(there)
        def _(peer=peer):
            pl.semaphore_signal(barrier, inc=1, device_id=peer, device_id_type=MESH)

    for at in range(2):
        @pl.when(jnp.logical_not(sides[at][0]))
        def _(at=at):
            for slot in range(STEPS + 1):
                halo[slot, at] = jnp.zeros((m, 1, cols), f32)

        @pl.when(jnp.logical_not(sides[2 + at][0]))
        def _(at=at):
            beyond[at] = jnp.zeros((slab, cols), f32)

    root[m] = jnp.zeros((slab, cols), f32)

    def xs_copy(slot, at):
        return pltpu.make_async_remote_copy(
            src_ref=edge.at[slot, at], dst_ref=halo.at[slot, 1 - at],
            send_sem=xs_send.at[slot, at], recv_sem=xs_recv.at[slot, 1 - at],
            device_id=sides[at][1], device_id_type=MESH,
        )

    def xs_start(slot):
        for at in range(2):
            @pl.when(sides[at][0])
            def _(at=at):
                xs_copy(slot, at).start()

    def xs_wait(slot):
        for at in range(2):
            @pl.when(sides[at][0])
            def _(at=at):
                xs_copy(slot, 1 - at).wait_recv()

    def ax_copy(at):
        return pltpu.make_async_remote_copy(
            src_ref=root.at[(0, m - 1)[at]], dst_ref=beyond.at[1 - at],
            send_sem=ax_send.at[at], recv_sem=ax_recv.at[1 - at],
            device_id=sides[2 + at][1], device_id_type=MESH,
        )

    def set_root(z):
        diffusivity = mask[z].astype(f32) * lookup(layer[z], diff_tab) * stiff[z]
        value = jnp.sqrt(diffusivity)
        root[z] = value
        edge[STEPS, 0, z] = value[0:1]
        edge[STEPS, 1, z] = value[slab - 1:slab]

    for load in tables + outer_loads:
        load.wait()
    set_root(0)
    set_root(m - 1)
    pl.semaphore_wait(barrier, sum(jnp.where(there, 1, 0) for there, _ in greeted))
    for at in range(2):
        @pl.when(sides[2 + at][0])
        def _(at=at):
            ax_copy(at).start()

    for load in inner_loads:
        load.wait()

    def root_body(z, carry):
        set_root(z)
        return carry

    lax.fori_loop(1, m - 1, root_body, 0, unroll=6)
    xs_start(STEPS)

    def factor_body(z, carry):
        excess, product, total = carry
        band = (RZ * root[z]) * root[z + 1]
        inverse = 1.0 / (excess + band)
        ratio_now = band * inverse
        scaled = product * inverse
        ratio[z] = ratio_now
        recip[z] = inverse
        prodr[z] = scaled
        return 1.0 + ratio_now * excess, product * ratio_now, total + product * scaled

    ones = jnp.ones((slab, cols), f32)
    _, _, total = lax.fori_loop(0, m, factor_body, (ones, ones, 0.0 * ones), unroll=8)
    sigma = recip[m - 1]
    ratio[m - 1] = sigma

    for at in range(2):
        @pl.when(sides[2 + at][0])
        def _(at=at):
            ax_copy(1 - at).wait_recv()

    band_low = RZ * beyond[0] * root[0]
    band_high = RZ * root[m - 1] * beyond[1]
    outer_band = jnp.where(low, band_low, band_high)
    middle[...] = jnp.where(low, band_high, band_low)
    scale = jnp.sqrt(outer_band)
    scales[...] = scale
    dev_c[0] = jnp.where(low, outer_band, 1.0) * total
    dev_c[1] = scale * prodr[m - 1]
    dev_c[2] = jnp.where(low, 1.0, outer_band) * sigma

    def mate_copy(src, dst, send, recv):
        return pltpu.make_async_remote_copy(
            src_ref=src, dst_ref=dst, send_sem=send, recv_sem=recv, device_id=mate, device_id_type=MESH
        )

    def pair_c_copy(group):
        return mate_copy(
            dev_c.at[:, lines(other, group)], pair_c.at[:, kept_ds(group)], pc_send.at[group], pc_recv.at[group]
        )

    def pair_v_copy(step, group):
        return mate_copy(
            dev_v.at[step, :, lines(other, group)], pair_v.at[step, :, kept_ds(group)],
            pv_send.at[step, group], pv_recv.at[step, group],
        )

    def back_copy(step, group, starts):
        return mate_copy(
            back_out.at[step, group], flow.at[step, :, lines(starts, group)],
            bk_send.at[step, group], bk_recv.at[step, group],
        )

    def far_copy(src, dst, send, recv, to):
        return pltpu.make_async_remote_copy(
            src_ref=src, dst_ref=dst, send_sem=send, recv_sem=recv,
            device_id={"ax": 2 * to + core}, device_id_type=MESH,
        )

    def chip_c_copy(rows, sender, to):
        return far_copy(
            chip_c.at[chip, rows], chip_c.at[sender, rows], cc_send.at[to], cc_recv.at[sender], to
        )

    def raw_copy(group, rows, sender, to):
        return far_copy(
            raw_v.at[chip, group, rows], raw_v.at[sender, group, rows],
            cv_send.at[0, group, to], cv_recv.at[0, group, sender], to,
        )

    def fold_copy(step, group, row, sender, to):
        return far_copy(
            fold_out.at[step, group, row], fold_v.at[step, sender, group],
            cv_send.at[step, group, to], cv_recv.at[step, group, sender], to,
        )

    def sent_rows(count, act):
        last = count - 1

        @pl.when(chip == 0)
        def _():
            act(pl.ds(last, 1))

        @pl.when(chip == chips - 1)
        def _():
            act(pl.ds(0, 1))

        @pl.when((chip > 0) & (chip < chips - 1))
        def _():
            act(pl.ds(0, count))

    def received_rows(count, sender):
        if sender == 0:
            return pl.ds(count - 1, 1)
        if sender == chips - 1:
            return pl.ds(0, 1)
        return pl.ds(0, count)

    def to_all(act):
        for there, to in far:
            @pl.when(there)
            def _(to=to):
                act(to)

    def from_all(act):
        for sender in range(chips):
            @pl.when(chip != sender)
            def _(sender=sender):
                act(sender)

    for group in range(2):
        pair_c_copy(group).start()

    col_at = lax.broadcasted_iota(jnp.int32, (slab, cols), 1)

    def plane_body(z, carry):
        value = root[z]
        scaled = SECTION_RATE * value
        plane[z] = scaled * pltpu.roll(value, 1, 0)
        side[z] = jnp.where(col_at == 0, 0.0, scaled * pltpu.roll(value, 1, 1))
        return carry

    lax.fori_loop(0, m, plane_body, 0, unroll=8)
    conc_load.wait()

    def copy_edges(z, carry):
        edge[0, 0, z] = state[z, 0:1]
        edge[0, 1, z] = state[z, slab - 1:slab]
        return carry

    lax.fori_loop(0, m, copy_edges, 0, unroll=8)
    xs_start(0)

    for group in range(2):
        pair_c_copy(group).wait_recv()
        at = kept(group)
        mine = [dev_c[row, lines(own, group)] for row in range(3)]
        his = [pair_c[row, at] for row in range(3)]
        tau_l, rho_l, sigma_l = [jnp.where(low, a, b) for a, b in zip(mine, his)]
        tau_u, rho_u, sigma_u = [jnp.where(low, b, a) for a, b in zip(mine, his)]
        band = middle[lines(own, group)]
        joint = band / (1.0 + band * (sigma_l + tau_u))
        link_l, link_u = rho_l * joint, rho_u * joint
        links[0, at], links[1, at], links[2, at] = joint, link_l, link_u
        chip_c[chip, 0, at] = tau_l - rho_l * link_l
        chip_c[chip, 1, at] = rho_l * link_u
        chip_c[chip, 2, at] = sigma_u - rho_u * link_u

    sent_rows(3, lambda rows: to_all(lambda to: chip_c_copy(rows, chip, to).start()))

    def fix_body(z, carry):
        scaled = SECTION_RATE * root[z]
        plane[z, 0:1] = scaled[0:1] * halo[STEPS, 0, z]
        shut[z] = scaled[slab - 1:slab] * halo[STEPS, 1, z]
        return carry

    def cell_body(z, carry):
        weight = mask[z].astype(f32)
        uptake[z] = weight * lookup(layer[z], upt_tab)
        source[z] = weight * source[z]
        return carry

    def forward(step, ranges):
        def body(z, carries):
            done = []
            for (lo, hi), (moved, first) in zip(ranges, carries):
                span = slice(lo, hi)
                size = hi - lo
                row = lax.broadcasted_iota(jnp.int32, (size, cols), 0)
                now = state[z, span]
                before = halo[step, 0, z] if lo == 0 else state[z, lo - 1:lo]
                above = jnp.where(row == 0, before, pltpu.roll(now, 1, 0))
                flux = plane[z, span] * (above - now)
                if hi == slab:
                    closing = shut[z] * (now[size - 1:size] - halo[step, 1, z])
                else:
                    closing = plane[z, hi:hi + 1] * (now[size - 1:size] - state[z, hi:hi + 1])
                below = jnp.where(row == size - 1, closing, pltpu.roll(flux, size - 1, 0))
                across = side[z, span] * (pltpu.roll(now, 1, 1) - now)
                explicit = now + ((flux - below) + (across - pltpu.roll(across, cols - 1, 1)))
                value = explicit + moved
                part[z, span] = recip[z, span] * value
                done.append((ratio[z, span] * value, first + prodr[z, span] * value))
            return tuple(done)

        zeros = [jnp.zeros((hi - lo, cols), f32) for lo, hi in ranges]
        sums = lax.fori_loop(0, m, body, tuple((zero, zero) for zero in zeros), unroll=8)
        for (lo, hi), (_, first) in zip(ranges, sums):
            span = slice(lo, hi)
            dev_v[step, 0, span] = jnp.where(low, scales[span], 1.0) * first
            dev_v[step, 1, span] = jnp.where(low, 1.0, scales[span]) * part[m - 1, span]

    def gather_coefficients():
        from_all(lambda sender: chip_c_copy(received_rows(3, sender), sender, sender).wait_recv())
        zero = jnp.zeros((half, cols), f32)
        left, right = [zero] * (chips + 1), [zero] * (chips + 1)
        solve_c[0, 0] = zero
        for at in range(chips - 1):
            if at == 0:
                left[1] = chip_c[0, 2]
            else:
                gain = chip_c[at, 1] / (1.0 + left[at] + chip_c[at, 0])
                solve_c[0, at] = gain
                left[at + 1] = chip_c[at, 2] - gain * chip_c[at, 1]
        for at in range(chips - 1, 0, -1):
            if at == chips - 1:
                right[at] = chip_c[at, 0]
            else:
                gain = chip_c[at, 1] / (1.0 + right[at + 1] + chip_c[at, 2])
                solve_c[1, at] = gain
                right[at] = chip_c[at, 0] - gain * chip_c[at, 1]
        solve_c[0, chips - 1] = own_gain(left[chips - 1], 0)
        solve_c[1, 0] = own_gain(right[1], 2)
        solve_c[1, chips - 1] = zero
        for at in range(chips + 1):
            solve_c[2, at] = 1.0 / (1.0 + left[at] + right[at]) if 0 < at < chips else zero

    def own_gain(response, row):
        return chip_c[chip, 1] / (1.0 + response + chip_c[chip, row])

    def combine(step, group):
        at = kept(group)
        pair_v_copy(step, group).wait_recv()
        mine = [dev_v[step, row, lines(own, group)] for row in range(2)]
        his = [pair_v[step, row, at] for row in range(2)]
        first_l, last_l = [jnp.where(low, a, b) for a, b in zip(mine, his)]
        first_u, last_u = [jnp.where(low, b, a) for a, b in zip(mine, his)]
        gap = last_l - first_u
        first = first_l - links[1, at] * gap
        last = last_u + links[2, at] * gap
        return links[0, at] * gap, first, last

    def send_raw(group, first, last):
        raw_v[chip, group, 0] = first
        raw_v[chip, group, 1] = last
        sent_rows(2, lambda rows: to_all(lambda to: raw_copy(group, rows, chip, to).start()))

    def send_folded(step, group, first, last):
        at = kept(group)
        fold_out[step, group, 0] = first - solve_c[1, chip, at] * last
        fold_out[step, group, 1] = last - solve_c[0, chip, at] * first

        def act(to):
            @pl.when(to > chip)
            def _():
                fold_copy(step, group, 1, chip, to).start()

            @pl.when(to < chip)
            def _():
                fold_copy(step, group, 0, chip, to).start()

        to_all(act)

    def interfaces(step, group, gap, first, last):
        at = kept(group)
        below = jnp.zeros((q, cols), f32)
        above = jnp.zeros((q, cols), f32)
        if step == 0:
            from_all(lambda sender: raw_copy(group, received_rows(2, sender), sender, sender).wait_recv())
            for sender in range(chips - 1):
                there = raw_v[sender, group, 1]
                if sender > 0:
                    there = there + solve_c[0, sender, at] * (below - raw_v[sender, group, 0])
                below = jnp.where(sender < chip, there, below)
            for sender in range(chips - 1, 0, -1):
                there = raw_v[sender, group, 0]
                if sender < chips - 1:
                    there = there - solve_c[1, sender, at] * (raw_v[sender, group, 1] - above)
                above = jnp.where(sender > chip, there, above)
        else:
            from_all(lambda sender: fold_copy(step, group, 0, sender, sender).wait_recv())
            for sender in range(chips - 1):
                there = fold_v[step, sender, group]
                if sender > 0:
                    there = there + solve_c[0, sender, at] * below
                below = jnp.where(sender < chip, there, below)
            for sender in range(chips - 1, 0, -1):
                there = fold_v[step, sender, group]
                if sender < chips - 1:
                    there = there + solve_c[1, sender, at] * above
                above = jnp.where(sender > chip, there, above)
        gain_up, gain_down = solve_c[0, chip, at], solve_c[1, chip, at]
        from_low = last + gain_up * (below - first)
        from_high = first - gain_down * (last - above)
        flow_low = (below - from_high) * solve_c[2, chip, at]
        flow_high = (from_low - above) * solve_c[2, chip + 1, at]
        flow_mid = gap + links[1, at] * flow_low + links[2, at] * flow_high
        flow[step, 0, lines(own, group)] = flow_mid
        flow[step, 1, lines(own, group)] = jnp.where(low, flow_low, flow_high)
        back_out[step, group, 0] = flow_mid
        back_out[step, group, 1] = jnp.where(low, flow_high, flow_low)
        back_copy(step, group, own).start()

    def backward(step, ranges, final):
        lows = []
        highs = []
        for lo, hi in ranges:
            span = slice(lo, hi)
            mid, outer = flow[step, 0, span], scales[span] * flow[step, 1, span]
            lows.append(jnp.where(low, outer, mid))
            highs.append(-jnp.where(low, mid, outer))

        def body(at, carries):
            z = m - 1 - at
            done = []
            for (lo, hi), entering, later in zip(ranges, lows, carries):
                span = slice(lo, hi)
                solved = part[z, span] + prodr[z, span] * entering + ratio[z, span] * later
                after = solved + (source[z, span] - uptake[z, span] * solved)
                if final:
                    out_ref[z, span] = after
                else:
                    state[z, span] = after
                    if lo == 0:
                        edge[step + 1, 0, z] = after[0:1]
                    if hi == slab:
                        edge[step + 1, 1, z] = after[hi - lo - 1:hi - lo]
                done.append(solved)
            return tuple(done)

        lax.fori_loop(0, m, body, tuple(highs), unroll=8)

    for step in range(STEPS):
        for group in range(2):
            if group == 1:
                if step == 0:
                    xs_wait(STEPS)
                    lax.fori_loop(0, m, fix_body, 0, unroll=8)
                xs_wait(step)
            forward(step, spans[group])
            pair_v_copy(step, group).start()
        found = []
        for group in range(2):
            found.append(combine(step, group))
            if step == 0:
                send_raw(group, *found[-1][1:])
            else:
                send_folded(step, group, *found[-1][1:])
        if step == 0:
            prod_load.wait()
            lax.fori_loop(0, m, cell_body, 0, unroll=8)
            gather_coefficients()
        for group in range(2):
            interfaces(step, group, *found[group])
        final = step == STEPS - 1
        if final:
            for group in range(2):
                back_copy(step, group, other).wait_recv()
                backward(step, spans[group], final)
        else:
            back_copy(step, 1, other).wait_recv()
            backward(step, ends, final)
            xs_start(step + 1)
            back_copy(step, 0, other).wait_recv()
            backward(step, inside, final)

    for at in range(2):
        @pl.when(sides[at][0])
        def _(at=at):
            for slot in range(STEPS + 1):
                xs_copy(slot, at).wait_send()

        @pl.when(sides[2 + at][0])
        def _(at=at):
            ax_copy(at).wait_send()

    sent_rows(3, lambda rows: to_all(lambda to: chip_c_copy(rows, chip, to).wait_send()))
    for group in range(2):
        pair_c_copy(group).wait_send()
        sent_rows(2, lambda rows, group=group: to_all(lambda to: raw_copy(group, rows, chip, to).wait_send()))
        for step in range(STEPS):
            pair_v_copy(step, group).wait_send()
            back_copy(step, group, own).wait_send()
            if step > 0:
                to_all(lambda to, step=step, group=group: fold_copy(step, group, 0, chip, to).wait_send())


def on_device(n_ax, n_xs, conc, mask, layer, stiff, prod, diff_tab, upt_tab):
    m, slab, cols = conc.shape
    chips = n_ax // 2
    half, q = slab // 2, slab // 4
    f32 = jnp.float32
    cells = pltpu.VMEM((m, slab, cols), f32)
    labels = pltpu.VMEM((m, slab, cols), jnp.int32)
    dma = pltpu.SemaphoreType.DMA
    vmem = lambda *shape: pltpu.VMEM(shape, f32)
    hbm_spec = pl.BlockSpec(memory_space=pltpu.HBM)
    return pl.pallas_call(
        functools.partial(kernel, n_ax, n_xs),
        out_shape=pltpu.VMEM((m, slab, cols), f32),
        in_specs=[hbm_spec] * 7,
        out_specs=pl.BlockSpec(memory_space=pltpu.VMEM),
        scratch_shapes=[
            pltpu.SMEM(diff_tab.shape, f32), pltpu.SMEM(upt_tab.shape, f32),
            labels, labels, cells, cells, cells, vmem(m + 1, slab, cols),
            cells, cells, cells, cells, cells, cells, cells,
            vmem(STEPS + 1, 2, m, 1, cols), vmem(STEPS + 1, 2, m, 1, cols), vmem(m, 1, cols),
            vmem(2, slab, cols), vmem(slab, cols), vmem(slab, cols),
            vmem(3, slab, cols), vmem(3, half, cols), vmem(chips, 3, half, cols),
            vmem(3, half, cols), vmem(3, chips + 1, half, cols),
            vmem(STEPS, 2, slab, cols), vmem(STEPS, 2, half, cols),
            vmem(chips, 2, 2, q, cols), vmem(STEPS, chips, 2, q, cols), vmem(STEPS, 2, 2, q, cols),
            vmem(STEPS, 2, slab, cols), vmem(STEPS, 2, 2, q, cols),
            dma((13,)), dma((STEPS + 1, 2)), dma((STEPS + 1, 2)), dma((2,)), dma((2,)),
            dma((2,)), dma((2,)), dma((STEPS, 2)), dma((STEPS, 2)), dma((STEPS, 2)), dma((STEPS, 2)),
            dma((chips,)), dma((chips,)), dma((STEPS, 2, chips)), dma((STEPS, 2, chips)),
        ],
        compiler_params=pltpu.CompilerParams(
            collective_id=0, has_side_effects=True, vmem_limit_bytes=56 * 1024 * 1024
        ),
    )(conc, mask, layer, stiff, prod, diff_tab, upt_tab)


def solution(mesh):
    cells = P("ax", "xs", None)
    return jax.shard_map(
        functools.partial(on_device, mesh.shape["ax"], mesh.shape["xs"]),
        mesh=mesh, in_specs=(cells,) * 5 + (P(), P()), out_specs=cells, check_vma=False,
    )
```

```python
import functools

import jax
import jax.numpy as jnp
from jax import lax
from jax.experimental import pallas as pl
from jax.experimental.pallas import tpu as pltpu
from jax.sharding import PartitionSpec as P

STEPS = 2
RZ = 3072
SECTION_RATE = 0.05
LOADS = 4
AHEAD = 4
GREET = 1
CONC_AT = 1
PROD_AT = 2
MESH = pl.DeviceIdType.MESH


def lookup(labels, table):
    found = jnp.full(labels.shape, table[0], jnp.float32)
    for index in range(1, len(table)):
        found = jnp.where(labels == index, table[index], found)
    return found


def kernel(
    n_ax, n_xs,
    conc_hbm, mask_hbm, layer_hbm, stiff_hbm, prod_hbm, diff_hbm, upt_hbm,
    state,
    diff_tab, upt_tab,
    mask_face, layer_face, stiff_face, face, mask_rim, layer_rim, stiff_rim, rim, mask, layer, stiff, source, root, ratio, recip, prodr, part, plane, side, keep,
    edge, halo, shut, beyond, scales, middle, dev_c, pair_c, chip_c, links, gain_up, gain_down, face_gain,
    dev_v, pair_v, raw_v, fold_v, fold_out, found, heard, flow, back_out,
    in_sem, xs_send, xs_recv, ax_send, ax_recv,
    pc_send, pc_recv, pv_send, pv_recv, bk_send, bk_recv, cc_send, cc_recv, cv_send, cv_recv,
):
    m, slab, cols = conc_hbm.shape
    chips = n_ax // 2
    half = slab // 2
    q = slab // 4
    f32 = jnp.float32
    me = lax.axis_index("ax")
    mx = lax.axis_index("xs")
    chip = lax.div(me, 2)
    core = lax.rem(me, 2)
    low = core == 0
    mate = {"ax": me + 1 - 2 * core}

    inside, ends = ((q, half + q),), ((0, q), (half + q, slab))

    def lines(mine, group):
        inner = jnp.where(low, q, half) if mine else jnp.where(low, half, q)
        outer = jnp.where(low, 0, half + q) if mine else jnp.where(low, half + q, 0)
        return pl.ds(pl.multiple_of(jnp.where(group == 0, inner, outer), 8), q)

    spans = (inside, ends)

    def kept(group):
        return pl.ds(pl.multiple_of(group * q, 8), q)

    def local(src, dst, at):
        return pltpu.make_async_copy(src, dst, in_sem.at[at])

    chunk = m // LOADS
    arrays = [
        (mask_hbm, mask, mask_face, mask_rim), (layer_hbm, layer, layer_face, layer_rim),
        (stiff_hbm, stiff, stiff_face, stiff_rim),
    ]
    tables = [local(diff_hbm, diff_tab, 0), local(upt_hbm, upt_tab, 1)]
    face_loads = [
        local(src.at[z], dst.at[k], 2 + 2 * at + k)
        for at, (src, _, dst, _) in enumerate(arrays) for k, z in enumerate((0, m - 1))
    ]
    rim_loads = [
        local(src.at[:, line], dst.at[k], 8 + 2 * at + k)
        for at, (src, _, _, dst) in enumerate(arrays) for k, line in enumerate((0, slab - 1))
    ]
    conc_load = local(conc_hbm, state, 14)
    prod_load = local(prod_hbm, source, 15)

    def part_loads(at):
        planes = pl.ds(at * chunk, chunk)
        return [
            local(src.at[planes], dst.at[planes], 16 + 3 * at + k) for k, (src, dst, _, _) in enumerate(arrays)
        ]

    sides = (
        (mx > 0, {"xs": mx - 1}),
        (mx < n_xs - 1, {"xs": mx + 1}),
        (me > 0, {"ax": me - 1}),
        (me < n_ax - 1, {"ax": me + 1}),
    )
    last_chip = chip == chips - 1
    between = (chip > 0) & (chip < chips - 1)
    peers = [lax.rem(chip + reach, chips) for reach in range(chips - 1, 0, -1)]
    greeted = list(sides) + [(True, {"ax": 2 * to + core}) for to in peers]
    barrier = pltpu.get_barrier_semaphore()
    for there, peer in greeted:
        @pl.when(there)
        def _(peer=peer):
            pl.semaphore_signal(barrier, inc=1, device_id=peer, device_id_type=MESH)

    for load in tables + part_loads(0) + face_loads + rim_loads:
        load.start()
    for at in range(1, AHEAD):
        for load in part_loads(at):
            load.start()

    for at in range(2):
        @pl.when(jnp.logical_not(sides[at][0]))
        def _(at=at):
            for slot in range(STEPS + 1):
                halo[slot, at] = jnp.zeros((m, 1, cols), f32)

        @pl.when(jnp.logical_not(sides[2 + at][0]))
        def _(at=at):
            beyond[at] = jnp.zeros((slab, cols), f32)

    root[m] = jnp.zeros((slab, cols), f32)

    def xs_copy(slot, at, src=None):
        return pltpu.make_async_remote_copy(
            src_ref=rim.at[at] if src is None else src, dst_ref=halo.at[slot, 1 - at, :, 0],
            send_sem=xs_send.at[slot, at], recv_sem=xs_recv.at[slot, 1 - at],
            device_id=sides[at][1], device_id_type=MESH,
        )

    def xs_start(slot, sources):
        for at in range(2):
            @pl.when(sides[at][0])
            def _(at=at):
                xs_copy(slot, at, sources[at]).start()

    def xs_wait(slot):
        for at in range(2):
            @pl.when(sides[at][0])
            def _(at=at):
                xs_copy(slot, 1 - at).wait_recv()

    def ax_copy(at):
        return pltpu.make_async_remote_copy(
            src_ref=face.at[at], dst_ref=beyond.at[1 - at],
            send_sem=ax_send.at[at], recv_sem=ax_recv.at[1 - at],
            device_id=sides[2 + at][1], device_id_type=MESH,
        )

    for load in tables:
        load.wait()
    scaled_table = [RZ * diff_tab[index] for index in range(diff_tab.shape[0])]

    def scaled_root(mask_now, layer_now, stiff_now):
        square = lookup(layer_now, scaled_table) * stiff_now
        return jnp.where(mask_now != 0, square * lax.rsqrt(square), 0.0)

    col_at = lax.broadcasted_iota(jnp.int32, (slab, cols), 1)

    def root_part(at, carry):
        @pl.when(at == GREET)
        def _():
            for load in face_loads + rim_loads:
                load.wait()
            for end in range(2):
                face[end] = scaled_root(mask_face[end], layer_face[end], stiff_face[end])
                rim[end] = scaled_root(mask_rim[end], layer_rim[end], stiff_rim[end])
            pl.semaphore_wait(barrier, sum(jnp.where(there, 1, 0) for there, _ in greeted))
            for way in range(2):
                @pl.when(sides[2 + way][0])
                def _(way=way):
                    ax_copy(way).start()
            xs_start(STEPS, [rim.at[0], rim.at[1]])
            xs_start(0, [conc_hbm.at[:, 0], conc_hbm.at[:, slab - 1]])

        for load in part_loads(at):
            load.wait()

        if AHEAD < LOADS:
            @pl.when(at + AHEAD < LOADS)
            def _():
                for load in part_loads(at + AHEAD):
                    load.start()

        @pl.when(at == CONC_AT)
        def _():
            conc_load.start()

        @pl.when(at == PROD_AT)
        def _():
            prod_load.start()

        for offset in range(chunk):
            z = at * chunk + offset
            value = scaled_root(mask[z], layer[z], stiff[z])
            root[z] = value
            scaled = (SECTION_RATE / RZ) * value
            plane[z] = scaled * pltpu.roll(value, 1, 0)
            side[z] = jnp.where(col_at == 0, 0.0, scaled * pltpu.roll(value, 1, 1))
        return carry

    lax.fori_loop(0, LOADS, root_part, 0)

    def factor_body(z, carry):
        excess, product, total = carry
        band = root[z] * root[z + 1]
        inverse = pl.reciprocal(excess + band, approx=True)
        ratio_now = band * inverse
        scaled = product * inverse
        ratio[z] = ratio_now
        recip[z] = inverse
        prodr[z] = scaled
        return 1.0 + ratio_now * excess, product * ratio_now, total + product * scaled

    ones = jnp.ones((slab, cols), f32)
    _, _, total = lax.fori_loop(0, m, factor_body, (ones, ones, 0.0 * ones), unroll=8)
    sigma = recip[m - 1]
    ratio[m - 1] = sigma

    for at in range(2):
        @pl.when(sides[2 + at][0])
        def _(at=at):
            ax_copy(1 - at).wait_recv()

    band_low = beyond[0] * root[0]
    band_high = root[m - 1] * beyond[1]
    outer_band = jnp.where(low, band_low, band_high)
    middle[...] = jnp.where(low, band_high, band_low)
    scale = jnp.sqrt(outer_band)
    scales[...] = scale
    dev_c[0] = jnp.where(low, outer_band, 1.0) * total
    dev_c[1] = scale * prodr[m - 1]
    dev_c[2] = jnp.where(low, 1.0, outer_band) * sigma

    def mate_copy(src, dst, send, recv):
        return pltpu.make_async_remote_copy(
            src_ref=src, dst_ref=dst, send_sem=send, recv_sem=recv, device_id=mate, device_id_type=MESH
        )

    def pair_c_copy(group):
        return mate_copy(
            dev_c.at[:, lines(False, group)], pair_c.at[:, kept(group)], pc_send.at[group], pc_recv.at[group]
        )

    def pair_v_copy(step, group):
        return mate_copy(
            dev_v.at[step, :, lines(False, group)], pair_v.at[step, :, kept(group)],
            pv_send.at[step, group], pv_recv.at[step, group],
        )

    def back_copy(step, group, mine):
        return mate_copy(
            back_out.at[step, group], flow.at[step, :, lines(mine, group)],
            bk_send.at[step, group], bk_recv.at[step, group],
        )

    def far_copy(src, dst, send, recv, to):
        return pltpu.make_async_remote_copy(
            src_ref=src, dst_ref=dst, send_sem=send, recv_sem=recv,
            device_id={"ax": 2 * to + core}, device_id_type=MESH,
        )

    def coef_copy(count, sender, to):
        rows = pl.ds(3 - count, count)
        return far_copy(
            chip_c.at[chip, rows], chip_c.at[sender, rows], cc_send.at[to], cc_recv.at[sender], to
        )

    def raw_copy(count, group, sender, to):
        rows = pl.ds(2 - count, count)
        return far_copy(
            raw_v.at[chip, group, rows], raw_v.at[sender, group, rows],
            cv_send.at[0, group, to], cv_recv.at[0, group, sender], to,
        )

    def fold_copy(step, group, sender, to):
        return far_copy(
            fold_out.at[step, group, jnp.where(to > chip, 1, 0)], fold_v.at[step, sender, group],
            cv_send.at[step, group, to], cv_recv.at[step, group, sender], to,
        )

    def to_peers(count, act):
        @pl.when(between)
        def _():
            for to in peers:
                act(count, to)

        @pl.when(jnp.logical_not(between))
        def _():
            for to in peers:
                act(1, to)

    def from_peers(count, act):
        for sender in range(chips):
            @pl.when(chip != sender)
            def _(sender=sender):
                act(count if 0 < sender < chips - 1 else 1, sender)

    def tau_of(at):
        return chip_c[at, 2 if at == chips - 1 else 1]

    def sigma_of(at):
        return chip_c[at, 1 if at == chips - 1 else 2]

    def loop_groups(act):
        def body(group, carry):
            act(group)
            return carry

        lax.fori_loop(0, 2, body, 0)

    loop_groups(lambda group: pair_c_copy(group).start())

    def combine_coefficients():
        def one(group):
            pair_c_copy(group).wait_recv()
            at = kept(group)
            mine = [dev_c[row, lines(True, group)] for row in range(3)]
            his = [pair_c[row, at] for row in range(3)]
            tau_l, rho_l, sigma_l = [jnp.where(low, a, b) for a, b in zip(mine, his)]
            tau_u, rho_u, sigma_u = [jnp.where(low, b, a) for a, b in zip(mine, his)]
            band = middle[lines(True, group)]
            joint = band * pl.reciprocal(1.0 + band * (sigma_l + tau_u), approx=True)
            link_l, link_u = rho_l * joint, rho_u * joint
            links[0, at], links[1, at], links[2, at] = joint, link_l, link_u
            tau, sigma = tau_l - rho_l * link_l, sigma_u - rho_u * link_u
            chip_c[chip, 0, at] = rho_l * link_u
            chip_c[chip, 1, at] = jnp.where(last_chip, sigma, tau)
            chip_c[chip, 2, at] = jnp.where(last_chip, tau, sigma)

        loop_groups(one)
        to_peers(3, lambda count, to: coef_copy(count, chip, to).start())

    def gather_coefficients():
        from_peers(3, lambda count, sender: coef_copy(count, sender, sender).wait_recv())
        zero = jnp.zeros((half, cols), f32)
        below, above = [zero] * (chips + 1), [zero] * (chips + 1)
        gain_up[0] = zero
        gain_up[chips - 1] = zero
        gain_down[0] = zero
        gain_down[chips - 1] = zero
        below[1] = sigma_of(0)
        for at in range(1, chips - 1):
            gain = chip_c[at, 0] * pl.reciprocal(1.0 + below[at] + tau_of(at), approx=True)
            gain_up[at] = gain
            below[at + 1] = sigma_of(at) - gain * chip_c[at, 0]
        above[chips - 1] = tau_of(chips - 1)
        for at in range(chips - 2, 0, -1):
            gain = chip_c[at, 0] * pl.reciprocal(1.0 + above[at + 1] + sigma_of(at), approx=True)
            gain_down[at] = gain
            above[at] = tau_of(at) - gain * chip_c[at, 0]
        face_gain[0] = zero
        face_gain[chips] = zero
        for at in range(1, chips):
            face_gain[at] = pl.reciprocal(1.0 + below[at] + above[at], approx=True)

    def fix_body(z, carry):
        scaled = (SECTION_RATE / RZ) * root[z]
        plane[z, 0:1] = scaled[0:1] * halo[STEPS, 0, z]
        shut[z] = scaled[slab - 1:slab] * halo[STEPS, 1, z]
        return carry

    keep_table = [1.0 - upt_tab[index] for index in range(upt_tab.shape[0])]

    def cell_body(z, carry):
        there = mask[z] != 0
        keep[z] = jnp.where(there, lookup(layer[z], keep_table), 1.0)
        source[z] = jnp.where(there, source[z], 0.0)
        return carry

    def forward(step, ranges):
        def body(z, carries):
            done = []
            for (lo, hi), (moved, first) in zip(ranges, carries):
                span = slice(lo, hi)
                size = hi - lo
                row = lax.broadcasted_iota(jnp.int32, (size, cols), 0)
                now = state[z, span]
                before = halo[step, 0, z] if lo == 0 else state[z, lo - 1:lo]
                above = jnp.where(row == 0, before, pltpu.roll(now, 1, 0))
                flux = plane[z, span] * (above - now)
                if hi == slab:
                    closing = shut[z] * (now[size - 1:size] - halo[step, 1, z])
                else:
                    closing = plane[z, hi:hi + 1] * (now[size - 1:size] - state[z, hi:hi + 1])
                below = jnp.where(row == size - 1, closing, pltpu.roll(flux, size - 1, 0))
                across = side[z, span] * (pltpu.roll(now, 1, 1) - now)
                explicit = now + ((flux - below) + (across - pltpu.roll(across, cols - 1, 1)))
                value = explicit + moved
                part[z, span] = recip[z, span] * value
                done.append((ratio[z, span] * value, first + prodr[z, span] * value))
            return tuple(done)

        zeros = [jnp.zeros((hi - lo, cols), f32) for lo, hi in ranges]
        sums = lax.fori_loop(0, m, body, tuple((zero, zero) for zero in zeros), unroll=8)
        for (lo, hi), (_, first) in zip(ranges, sums):
            span = slice(lo, hi)
            dev_v[step, 0, span] = jnp.where(low, scales[span], 1.0) * first
            dev_v[step, 1, span] = jnp.where(low, 1.0, scales[span]) * part[m - 1, span]

    def combine(step, group):
        at = kept(group)
        pair_v_copy(step, group).wait_recv()
        mine = [dev_v[step, row, lines(True, group)] for row in range(2)]
        his = [pair_v[step, row, at] for row in range(2)]
        first_l, last_l = [jnp.where(low, a, b) for a, b in zip(mine, his)]
        first_u, last_u = [jnp.where(low, b, a) for a, b in zip(mine, his)]
        gap = last_l - first_u
        first = first_l - links[1, at] * gap
        last = last_u + links[2, at] * gap
        found[0, at], found[1, at], found[2, at] = links[0, at] * gap, first, last

        if step == 0:
            raw_v[chip, group, 0] = jnp.where(last_chip, last, first)
            raw_v[chip, group, 1] = jnp.where(last_chip, first, last)
            to_peers(2, lambda count, to: raw_copy(count, group, chip, to).start())

        if step > 0:
            fold_out[step, group, 0] = first - gain_down[chip, at] * last
            fold_out[step, group, 1] = last - gain_up[chip, at] * first
            for to in peers:
                fold_copy(step, group, chip, to).start()

    def interfaces(step, group):
        at = kept(group)

        if step == 0:
            from_peers(2, lambda count, sender: raw_copy(count, group, sender, sender).wait_recv())
            below = jnp.zeros((q, cols), f32)
            above = jnp.zeros((q, cols), f32)
            for sender in range(chips - 1):
                there = raw_v[sender, group, 1]
                if sender > 0:
                    there = there + gain_up[sender, at] * (below - raw_v[sender, group, 0])
                below = jnp.where(sender < chip, there, below)
            for sender in range(chips - 1, 0, -1):
                if sender == chips - 1:
                    there = raw_v[sender, group, 1]
                else:
                    there = raw_v[sender, group, 0] - gain_down[sender, at] * (raw_v[sender, group, 1] - above)
                above = jnp.where(sender > chip, there, above)
            heard[0], heard[1] = below, above

        if step > 0:
            for sender in peers:
                fold_copy(step, group, sender, sender).wait_recv()
            below = jnp.zeros((q, cols), f32)
            above = jnp.zeros((q, cols), f32)
            for sender in range(chips - 1):
                there = fold_v[step, sender, group] + gain_up[sender, at] * below
                below = jnp.where(sender < chip, there, below)
            for sender in range(chips - 1, 0, -1):
                there = fold_v[step, sender, group] + gain_down[sender, at] * above
                above = jnp.where(sender > chip, there, above)
            heard[0], heard[1] = below, above

        below, above = heard[0], heard[1]
        gap, first, last = found[0, at], found[1, at], found[2, at]
        from_low = last + gain_up[chip, at] * (below - first)
        from_high = first - gain_down[chip, at] * (last - above)
        flow_low = (below - from_high) * face_gain[chip, at]
        flow_high = (from_low - above) * face_gain[chip + 1, at]
        flow_mid = gap + links[1, at] * flow_low + links[2, at] * flow_high
        flow[step, 0, lines(True, group)] = flow_mid
        flow[step, 1, lines(True, group)] = jnp.where(low, flow_low, flow_high)
        back_out[step, group, 0] = flow_mid
        back_out[step, group, 1] = jnp.where(low, flow_high, flow_low)
        back_copy(step, group, True).start()

    def backward(step, ranges):
        lows = []
        highs = []
        for lo, hi in ranges:
            span = slice(lo, hi)
            mid, outer = flow[step, 0, span], scales[span] * flow[step, 1, span]
            lows.append(jnp.where(low, outer, mid))
            highs.append(-jnp.where(low, mid, outer))

        def body(at, carries):
            z = m - 1 - at
            done = []
            for (lo, hi), entering, later in zip(ranges, lows, carries):
                span = slice(lo, hi)
                solved = part[z, span] + prodr[z, span] * entering + ratio[z, span] * later
                after = keep[z, span] * solved + source[z, span]
                state[z, span] = after
                if lo == 0:
                    edge[step, 0, z] = after[0:1]
                if hi == slab:
                    edge[step, 1, z] = after[hi - lo - 1:hi - lo]
                done.append(solved)
            return tuple(done)

        lax.fori_loop(0, m, body, tuple(highs), unroll=8)

    prod_load.wait()
    lax.fori_loop(0, m, cell_body, 0, unroll=8)
    xs_wait(STEPS)
    lax.fori_loop(0, m, fix_body, 0, unroll=8)
    combine_coefficients()
    conc_load.wait()

    for step in range(STEPS):
        order = (1, 0) if step == 0 else (0, 1)
        for group in order:
            if group == 1:
                xs_wait(step)
            forward(step, spans[group])
            pair_v_copy(step, group).start()
            if step > 0:
                combine(step, group)
        if step == 0:
            for group in order:
                combine(step, group)
            gather_coefficients()
        for group in order:
            if step == 0 or group == 0:
                interfaces(step, group)
            if step > 0 and group == 0:
                interfaces(step, 1)
            back_copy(step, group, False).wait_recv()
            backward(step, spans[group])
            if group == 1 and step < STEPS - 1:
                xs_start(step + 1, [edge.at[step, at, :, 0] for at in range(2)])

    for at in range(2):
        @pl.when(sides[at][0])
        def _(at=at):
            for slot in range(STEPS + 1):
                xs_copy(slot, at).wait_send()

        @pl.when(sides[2 + at][0])
        def _(at=at):
            ax_copy(at).wait_send()

    to_peers(3, lambda count, to: coef_copy(count, chip, to).wait_send())

    def finish(group):
        pair_c_copy(group).wait_send()
        to_peers(2, lambda count, to: raw_copy(count, group, chip, to).wait_send())
        for step in range(STEPS):
            pair_v_copy(step, group).wait_send()
            back_copy(step, group, True).wait_send()
            if step > 0:
                for to in peers:
                    fold_copy(step, group, chip, to).wait_send()

    loop_groups(finish)


def on_device(n_ax, n_xs, conc, mask, layer, stiff, prod, diff_tab, upt_tab):
    m, slab, cols = conc.shape
    chips = n_ax // 2
    half, q = slab // 2, slab // 4
    f32 = jnp.float32
    cells = pltpu.VMEM((m, slab, cols), f32)
    labels = pltpu.VMEM((m, slab, cols), jnp.int32)
    dma = pltpu.SemaphoreType.DMA
    vmem = lambda *shape: pltpu.VMEM(shape, f32)
    hbm_spec = pl.BlockSpec(memory_space=pltpu.HBM)
    return pl.pallas_call(
        functools.partial(kernel, n_ax, n_xs),
        out_shape=pltpu.VMEM((m, slab, cols), f32),
        in_specs=[hbm_spec] * 7,
        out_specs=pl.BlockSpec(memory_space=pltpu.VMEM),
        scratch_shapes=[
            pltpu.SMEM(diff_tab.shape, f32), pltpu.SMEM(upt_tab.shape, f32),
            pltpu.VMEM((2, slab, cols), jnp.int32), pltpu.VMEM((2, slab, cols), jnp.int32),
            vmem(2, slab, cols), vmem(2, slab, cols),
            pltpu.VMEM((2, m, cols), jnp.int32), pltpu.VMEM((2, m, cols), jnp.int32),
            vmem(2, m, cols), vmem(2, m, cols),
            labels, labels, cells, cells, vmem(m + 1, slab, cols),
            cells, cells, cells, cells, cells, cells, cells,
            vmem(STEPS, 2, m, 1, cols), vmem(STEPS + 1, 2, m, 1, cols), vmem(m, 1, cols),
            vmem(2, slab, cols), vmem(slab, cols), vmem(slab, cols),
            vmem(3, slab, cols), vmem(3, half, cols), vmem(chips, 3, half, cols),
            vmem(3, half, cols), vmem(chips, half, cols), vmem(chips, half, cols), vmem(chips + 1, half, cols),
            vmem(STEPS, 2, slab, cols), vmem(STEPS, 2, half, cols),
            vmem(chips, 2, 2, q, cols), vmem(STEPS, chips, 2, q, cols), vmem(STEPS, 2, 2, q, cols),
            vmem(3, half, cols), vmem(2, q, cols),
            vmem(STEPS, 2, slab, cols), vmem(STEPS, 2, 2, q, cols),
            dma((16 + 3 * LOADS,)), dma((STEPS + 1, 2)), dma((STEPS + 1, 2)), dma((2,)), dma((2,)),
            dma((2,)), dma((2,)), dma((STEPS, 2)), dma((STEPS, 2)), dma((STEPS, 2)), dma((STEPS, 2)),
            dma((chips,)), dma((chips,)), dma((STEPS, 2, chips)), dma((STEPS, 2, chips)),
        ],
        compiler_params=pltpu.CompilerParams(
            collective_id=0, has_side_effects=True, vmem_limit_bytes=56 * 1024 * 1024
        ),
    )(conc, mask, layer, stiff, prod, diff_tab, upt_tab)


def solution(mesh):
    cells = P("ax", "xs", None)
    return jax.shard_map(
        functools.partial(on_device, mesh.shape["ax"], mesh.shape["xs"]),
        mesh=mesh, in_specs=(cells,) * 5 + (P(), P()), out_specs=cells, check_vma=False,
    )
```

```python
import functools

import jax
import jax.numpy as jnp
from jax import lax
from jax.experimental import pallas as pl
from jax.experimental.pallas import tpu as pltpu
from jax.sharding import PartitionSpec as P

STEPS = 2
RZ = 3072
SECTION_RATE = 0.05
LOADS = 4
AHEAD = 4
GREET = 1
CONC_AT = 1
PROD_AT = 2
MESH = pl.DeviceIdType.MESH


def lookup(labels, table):
    found = jnp.full(labels.shape, table[0], jnp.float32)
    for index in range(1, len(table)):
        found = jnp.where(labels == index, table[index], found)
    return found


def kernel(
    n_ax, n_xs,
    conc_hbm, mask_hbm, layer_hbm, stiff_hbm, prod_hbm, diff_hbm, upt_hbm,
    state,
    diff_tab, upt_tab,
    mask_face, layer_face, stiff_face, face, mask_rim, layer_rim, stiff_rim, rim, mask, layer, stiff, source, root, ratio, recip, prodr, part, w_lower, w_upper, w_left, w_right, centre, keep,
    edge, halo, beyond, mate_face, dev_c, pair_c, chip_c, links, gain_up, gain_down, face_gain,
    dev_v, pair_v, raw_v, fold_v, fold_out, found, heard, flow, back_out,
    in_sem, xs_send, xs_recv, ax_send, ax_recv, face_sem,
    pc_send, pc_recv, pv_send, pv_recv, bk_send, bk_recv, cc_send, cc_recv, cv_send, cv_recv,
):
    m, slab, cols = conc_hbm.shape
    chips = n_ax // 2
    half = slab // 2
    q = slab // 4
    f32 = jnp.float32
    me = lax.axis_index("ax")
    mx = lax.axis_index("xs")
    chip = lax.div(me, 2)
    core = lax.rem(me, 2)
    low = core == 0
    mate = {"ax": me + 1 - 2 * core}

    inside, ends = ((q, half + q),), ((0, q), (half + q, slab))

    def lines(mine, group):
        inner = jnp.where(low, q, half) if mine else jnp.where(low, half, q)
        outer = jnp.where(low, 0, half + q) if mine else jnp.where(low, half + q, 0)
        return pl.ds(pl.multiple_of(jnp.where(group == 0, inner, outer), 8), q)

    spans = (inside, ends)

    def halfway(group):
        return pl.ds(pl.multiple_of(jnp.where(low == (group == 0), q, 0), 8), q)

    def kept(group):
        return pl.ds(pl.multiple_of(group * q, 8), q)

    def local(src, dst, at):
        return pltpu.make_async_copy(src, dst, in_sem.at[at])

    chunk = m // LOADS
    arrays = [
        (mask_hbm, mask, mask_face, mask_rim), (layer_hbm, layer, layer_face, layer_rim),
        (stiff_hbm, stiff, stiff_face, stiff_rim),
    ]
    tables = [local(diff_hbm, diff_tab, 0), local(upt_hbm, upt_tab, 1)]
    face_loads = [
        local(src.at[z], dst.at[k], 2 + 2 * at + k)
        for at, (src, _, dst, _) in enumerate(arrays) for k, z in enumerate((0, m - 1))
    ]
    rim_loads = [
        local(src.at[:, line], dst.at[k], 8 + 2 * at + k)
        for at, (src, _, _, dst) in enumerate(arrays) for k, line in enumerate((0, slab - 1))
    ]
    conc_load = local(conc_hbm, state, 14)
    prod_load = local(prod_hbm, source, 15)

    def part_loads(at):
        planes = pl.ds(at * chunk, chunk)
        return [
            local(src.at[planes], dst.at[planes], 16 + 3 * at + k) for k, (src, dst, _, _) in enumerate(arrays)
        ]

    sides = (
        (mx > 0, {"xs": mx - 1}),
        (mx < n_xs - 1, {"xs": mx + 1}),
        (me > 0, {"ax": me - 1}),
        (me < n_ax - 1, {"ax": me + 1}),
    )
    last_chip = chip == chips - 1
    between = (chip > 0) & (chip < chips - 1)
    peers = [lax.rem(chip + reach, chips) for reach in range(1, chips)]
    greeted = list(sides) + [(True, {"ax": 2 * to + core}) for to in peers]
    barrier = pltpu.get_barrier_semaphore()
    for there, peer in greeted:
        @pl.when(there)
        def _(peer=peer):
            pl.semaphore_signal(barrier, inc=1, device_id=peer, device_id_type=MESH)

    for load in tables + part_loads(0) + face_loads + rim_loads:
        load.start()
    for at in range(1, AHEAD):
        for load in part_loads(at):
            load.start()

    for at in range(2):
        @pl.when(jnp.logical_not(sides[at][0]))
        def _(at=at):
            for slot in range(STEPS + 1):
                halo[slot, at] = jnp.zeros((m, 1, cols), f32)

        @pl.when((chip == 0) if at == 0 else (chip == chips - 1))
        def _(at=at):
            beyond[at] = jnp.zeros((half, cols), f32)

    root[m] = jnp.zeros((slab, cols), f32)

    def xs_copy(slot, at, src=None):
        return pltpu.make_async_remote_copy(
            src_ref=rim.at[at] if src is None else src, dst_ref=halo.at[slot, 1 - at, :, 0],
            send_sem=xs_send.at[slot, at], recv_sem=xs_recv.at[slot, 1 - at],
            device_id=sides[at][1], device_id_type=MESH,
        )

    def xs_start(slot, sources):
        for at in range(2):
            @pl.when(sides[at][0])
            def _(at=at):
                xs_copy(slot, at, sources[at]).start()

    def xs_wait(slot):
        for at in range(2):
            @pl.when(sides[at][0])
            def _(at=at):
                xs_copy(slot, 1 - at).wait_recv()

    def ax_copy(to):
        step_to = jnp.where(low, -1, 1)
        return pltpu.make_async_remote_copy(
            src_ref=face.at[core, pl.ds(to * half, half)], dst_ref=beyond.at[1 - core],
            send_sem=ax_send.at[to], recv_sem=ax_recv.at[1 - core],
            device_id={"ax": 2 * (chip + step_to) + to}, device_id_type=MESH,
        )

    def ax_landed(at):
        return pltpu.make_async_remote_copy(
            src_ref=face.at[0, pl.ds(0, half)], dst_ref=beyond.at[at],
            send_sem=ax_send.at[0], recv_sem=ax_recv.at[at], device_id=mate, device_id_type=MESH,
        )

    def face_copy():
        return pltpu.make_async_remote_copy(
            src_ref=face.at[:, pl.ds(pl.multiple_of((1 - core) * half, 8), half)], dst_ref=mate_face,
            send_sem=face_sem.at[0], recv_sem=face_sem.at[1], device_id=mate, device_id_type=MESH,
        )

    has_outer = jnp.where(low, chip > 0, chip < chips - 1)

    for load in tables:
        load.wait()
    scaled_table = [RZ * diff_tab[index] for index in range(diff_tab.shape[0])]

    def scaled_root(mask_now, layer_now, stiff_now):
        square = lookup(layer_now, scaled_table) * stiff_now
        return jnp.where(mask_now != 0, square * lax.rsqrt(square), 0.0)

    row_at = lax.broadcasted_iota(jnp.int32, (slab, cols), 0)
    col_at = lax.broadcasted_iota(jnp.int32, (slab, cols), 1)

    def root_part(at, carry):
        @pl.when(at == GREET)
        def _():
            for load in face_loads + rim_loads:
                load.wait()
            for end in range(2):
                face[end] = scaled_root(mask_face[end], layer_face[end], stiff_face[end])
                rim[end] = scaled_root(mask_rim[end], layer_rim[end], stiff_rim[end])
            pl.semaphore_wait(barrier, sum(jnp.where(there, 1, 0) for there, _ in greeted))
            @pl.when(has_outer)
            def _():
                for to in range(2):
                    ax_copy(to).start()

            face_copy().start()
            xs_start(STEPS, [rim.at[0], rim.at[1]])
            xs_start(0, [conc_hbm.at[:, 0], conc_hbm.at[:, slab - 1]])

        for load in part_loads(at):
            load.wait()

        if AHEAD < LOADS:
            @pl.when(at + AHEAD < LOADS)
            def _():
                for load in part_loads(at + AHEAD):
                    load.start()

        @pl.when(at == CONC_AT)
        def _():
            conc_load.start()

        @pl.when(at == PROD_AT)
        def _():
            prod_load.start()

        for offset in range(chunk):
            z = at * chunk + offset
            value = scaled_root(mask[z], layer[z], stiff[z])
            root[z] = value
        return carry

    lax.fori_loop(0, LOADS, root_part, 0)

    def factor_body(z, carry):
        excess, product, total = carry
        band = root[z] * root[z + 1]
        inverse = pl.reciprocal(excess + band, approx=True)
        ratio_now = band * inverse
        scaled = product * inverse
        ratio[z] = ratio_now
        recip[z] = inverse
        prodr[z] = scaled
        return 1.0 + ratio_now * excess, product * ratio_now, total + product * scaled

    ones = jnp.ones((slab, cols), f32)
    _, _, total = lax.fori_loop(0, m, factor_body, (ones, ones, 0.0 * ones), unroll=8)
    sigma = recip[m - 1]
    ratio[m - 1] = sigma

    dev_c[0] = total
    dev_c[1] = prodr[m - 1]
    dev_c[2] = sigma

    def weight_body(z, carry):
        value = root[z]
        scaled = (SECTION_RATE / RZ) * value
        to_lower = jnp.where(row_at == 0, 0.0, scaled * pltpu.roll(value, 1, 0))
        to_left = jnp.where(col_at == 0, 0.0, scaled * pltpu.roll(value, 1, 1))
        to_upper = pltpu.roll(to_lower, slab - 1, 0)
        to_right = pltpu.roll(to_left, cols - 1, 1)
        w_lower[z], w_upper[z], w_left[z], w_right[z] = to_lower, to_upper, to_left, to_right
        centre[z] = 1.0 - ((to_lower + to_upper) + (to_left + to_right))
        return carry

    def mate_copy(src, dst, send, recv):
        return pltpu.make_async_remote_copy(
            src_ref=src, dst_ref=dst, send_sem=send, recv_sem=recv, device_id=mate, device_id_type=MESH
        )

    def pair_c_copy(group):
        return mate_copy(
            dev_c.at[:, lines(False, group)], pair_c.at[:, kept(group)], pc_send.at[group], pc_recv.at[group]
        )

    def pair_v_copy(step, group):
        return mate_copy(
            dev_v.at[step, :, lines(False, group)], pair_v.at[step, :, kept(group)],
            pv_send.at[step, group], pv_recv.at[step, group],
        )

    def back_copy(step, group, mine):
        return mate_copy(
            back_out.at[step, group], flow.at[step, :, lines(mine, group)],
            bk_send.at[step, group], bk_recv.at[step, group],
        )

    def far_copy(src, dst, send, recv, to):
        return pltpu.make_async_remote_copy(
            src_ref=src, dst_ref=dst, send_sem=send, recv_sem=recv,
            device_id={"ax": 2 * to + core}, device_id_type=MESH,
        )

    def coef_copy(count, sender, to):
        rows = pl.ds(3 - count, count)
        return far_copy(
            chip_c.at[chip, rows], chip_c.at[sender, rows], cc_send.at[to], cc_recv.at[sender], to
        )

    def raw_copy(count, group, sender, to):
        rows = pl.ds(2 - count, count)
        return far_copy(
            raw_v.at[chip, group, rows], raw_v.at[sender, group, rows],
            cv_send.at[0, group, to], cv_recv.at[0, group, sender], to,
        )

    def fold_copy(step, group, sender, to):
        return far_copy(
            fold_out.at[step, group, jnp.where(to > chip, 1, 0)], fold_v.at[step, sender, group],
            cv_send.at[step, group, to], cv_recv.at[step, group, sender], to,
        )

    def to_peers(count, act):
        @pl.when(between)
        def _():
            for to in peers:
                act(count, to)

        @pl.when(jnp.logical_not(between))
        def _():
            for to in peers:
                act(1, to)

    def from_peers(count, act):
        for sender in range(chips):
            @pl.when(chip != sender)
            def _(sender=sender):
                act(count if 0 < sender < chips - 1 else 1, sender)

    def tau_of(at):
        return chip_c[at, 2 if at == chips - 1 else 1]

    def sigma_of(at):
        return chip_c[at, 1 if at == chips - 1 else 2]

    def loop_groups(act):
        def body(group, carry):
            act(group)
            return carry

        lax.fori_loop(0, 2, body, 0)

    loop_groups(lambda group: pair_c_copy(group).start())
    lax.fori_loop(0, m, weight_body, 0, unroll=8)

    def combine_coefficients():
        def one(group):
            pair_c_copy(group).wait_recv()
            at = kept(group)
            mine = [dev_c[row, lines(True, group)] for row in range(3)]
            his = [pair_c[row, at] for row in range(3)]
            tau_l, rho_l, sigma_l = [jnp.where(low, a, b) for a, b in zip(mine, his)]
            tau_u, rho_u, sigma_u = [jnp.where(low, b, a) for a, b in zip(mine, his)]
            near = halfway(group)
            face_l, face_u = [
                [jnp.where(low == lower, face[k, lines(True, group)], mate_face[k, near]) for k in range(2)]
                for lower in (True, False)
            ]
            band = face_l[1] * face_u[0]
            joint = band * pl.reciprocal(1.0 + band * (sigma_l + tau_u), approx=True)
            link_l, link_u = rho_l * joint, rho_u * joint
            band_low, band_high = beyond[0, near] * face_l[0], face_u[1] * beyond[1, near]
            scale_low, scale_high = jnp.sqrt(band_low), jnp.sqrt(band_high)
            links[0, at], links[1, at], links[2, at] = joint, link_l, link_u
            links[3, at], links[4, at] = scale_low, scale_high
            tau, sigma = band_low * (tau_l - rho_l * link_l), band_high * (sigma_u - rho_u * link_u)
            chip_c[chip, 0, at] = (scale_low * scale_high) * (rho_l * link_u)
            chip_c[chip, 1, at] = jnp.where(last_chip, sigma, tau)
            chip_c[chip, 2, at] = jnp.where(last_chip, tau, sigma)

        for at in range(2):
            @pl.when((chip > 0) if at == 0 else (chip < chips - 1))
            def _(at=at):
                ax_landed(at).wait_recv()

        face_copy().wait_recv()
        loop_groups(one)
        to_peers(3, lambda count, to: coef_copy(count, chip, to).start())

    def gather_coefficients():
        from_peers(3, lambda count, sender: coef_copy(count, sender, sender).wait_recv())
        zero = jnp.zeros((half, cols), f32)
        below, above = [zero] * (chips + 1), [zero] * (chips + 1)
        gain_up[0] = zero
        gain_up[chips - 1] = zero
        gain_down[0] = zero
        gain_down[chips - 1] = zero
        below[1] = sigma_of(0)
        for at in range(1, chips - 1):
            gain = chip_c[at, 0] * pl.reciprocal(1.0 + below[at] + tau_of(at), approx=True)
            gain_up[at] = gain
            below[at + 1] = sigma_of(at) - gain * chip_c[at, 0]
        above[chips - 1] = tau_of(chips - 1)
        for at in range(chips - 2, 0, -1):
            gain = chip_c[at, 0] * pl.reciprocal(1.0 + above[at + 1] + sigma_of(at), approx=True)
            gain_down[at] = gain
            above[at] = tau_of(at) - gain * chip_c[at, 0]
        face_gain[0] = zero
        face_gain[chips] = zero
        for at in range(1, chips):
            face_gain[at] = pl.reciprocal(1.0 + below[at] + above[at], approx=True)

    def fix_body(z, carry):
        first, last = slice(0, 1), slice(slab - 1, slab)
        to_lower = (SECTION_RATE / RZ) * root[z, first] * halo[STEPS, 0, z]
        to_upper = (SECTION_RATE / RZ) * root[z, last] * halo[STEPS, 1, z]
        w_lower[z, first] = to_lower
        w_upper[z, last] = to_upper
        centre[z, first] = centre[z, first] - to_lower
        centre[z, last] = centre[z, last] - to_upper
        return carry

    keep_table = [1.0 - upt_tab[index] for index in range(upt_tab.shape[0])]

    def cell_body(z, carry):
        there = mask[z] != 0
        keep[z] = jnp.where(there, lookup(layer[z], keep_table), 1.0)
        source[z] = jnp.where(there, source[z], 0.0)
        return carry

    def forward(step, ranges):
        def body(z, carries):
            done = []
            for (lo, hi), (moved, first) in zip(ranges, carries):
                span = slice(lo, hi)
                size = hi - lo
                row = lax.broadcasted_iota(jnp.int32, (size, cols), 0)
                now = state[z, span]
                before = halo[step, 0, z] if lo == 0 else state[z, lo - 1:lo]
                behind = halo[step, 1, z] if hi == slab else state[z, hi:hi + 1]
                lower = jnp.where(row == 0, before, pltpu.roll(now, 1, 0))
                upper = jnp.where(row == size - 1, behind, pltpu.roll(now, size - 1, 0))
                across = w_left[z, span] * pltpu.roll(now, 1, 1) + w_right[z, span] * pltpu.roll(now, cols - 1, 1)
                along = w_lower[z, span] * lower + w_upper[z, span] * upper
                explicit = (centre[z, span] * now + along) + across
                value = explicit + moved
                part[z, span] = recip[z, span] * value
                done.append((ratio[z, span] * value, first + prodr[z, span] * value))
            return tuple(done)

        zeros = [jnp.zeros((hi - lo, cols), f32) for lo, hi in ranges]
        sums = lax.fori_loop(0, m, body, tuple((zero, zero) for zero in zeros), unroll=16)
        for (lo, hi), (_, first) in zip(ranges, sums):
            span = slice(lo, hi)
            dev_v[step, 0, span] = first
            dev_v[step, 1, span] = part[m - 1, span]

    def combine(step, group):
        at = kept(group)
        pair_v_copy(step, group).wait_recv()
        mine = [dev_v[step, row, lines(True, group)] for row in range(2)]
        his = [pair_v[step, row, at] for row in range(2)]
        first_l, last_l = [jnp.where(low, a, b) for a, b in zip(mine, his)]
        first_u, last_u = [jnp.where(low, b, a) for a, b in zip(mine, his)]
        gap = last_l - first_u
        first = links[3, at] * (first_l - links[1, at] * gap)
        last = links[4, at] * (last_u + links[2, at] * gap)
        found[0, at], found[1, at], found[2, at] = links[0, at] * gap, first, last

        if step == 0:
            raw_v[chip, group, 0] = jnp.where(last_chip, last, first)
            raw_v[chip, group, 1] = jnp.where(last_chip, first, last)
            to_peers(2, lambda count, to: raw_copy(count, group, chip, to).start())

        if step > 0:
            fold_out[step, group, 0] = first - gain_down[chip, at] * last
            fold_out[step, group, 1] = last - gain_up[chip, at] * first
            for to in peers:
                fold_copy(step, group, chip, to).start()

    def interfaces(step, group):
        at = kept(group)

        if step == 0:
            from_peers(2, lambda count, sender: raw_copy(count, group, sender, sender).wait_recv())
            below = jnp.zeros((q, cols), f32)
            above = jnp.zeros((q, cols), f32)
            for sender in range(chips - 1):
                there = raw_v[sender, group, 1]
                if sender > 0:
                    there = there + gain_up[sender, at] * (below - raw_v[sender, group, 0])
                below = jnp.where(sender < chip, there, below)
            for sender in range(chips - 1, 0, -1):
                if sender == chips - 1:
                    there = raw_v[sender, group, 1]
                else:
                    there = raw_v[sender, group, 0] - gain_down[sender, at] * (raw_v[sender, group, 1] - above)
                above = jnp.where(sender > chip, there, above)
            heard[0], heard[1] = below, above

        if step > 0:
            for sender in peers:
                fold_copy(step, group, sender, sender).wait_recv()
            below = jnp.zeros((q, cols), f32)
            above = jnp.zeros((q, cols), f32)
            for sender in range(chips - 1):
                there = fold_v[step, sender, group] + gain_up[sender, at] * below
                below = jnp.where(sender < chip, there, below)
            for sender in range(chips - 1, 0, -1):
                there = fold_v[step, sender, group] + gain_down[sender, at] * above
                above = jnp.where(sender > chip, there, above)
            heard[0], heard[1] = below, above

        below, above = heard[0], heard[1]
        gap, first, last = found[0, at], found[1, at], found[2, at]
        from_low = last + gain_up[chip, at] * (below - first)
        from_high = first - gain_down[chip, at] * (last - above)
        flow_low = (below - from_high) * face_gain[chip, at] * links[3, at]
        flow_high = (from_low - above) * face_gain[chip + 1, at] * links[4, at]
        flow_mid = gap + links[1, at] * flow_low + links[2, at] * flow_high
        flow[step, 0, lines(True, group)] = flow_mid
        flow[step, 1, lines(True, group)] = jnp.where(low, flow_low, flow_high)
        back_out[step, group, 0] = flow_mid
        back_out[step, group, 1] = jnp.where(low, flow_high, flow_low)
        back_copy(step, group, True).start()

    def backward(step, ranges):
        lows = []
        highs = []
        for lo, hi in ranges:
            span = slice(lo, hi)
            mid, outer = flow[step, 0, span], flow[step, 1, span]
            lows.append(jnp.where(low, outer, mid))
            highs.append(-jnp.where(low, mid, outer))

        def body(at, carries):
            z = m - 1 - at
            done = []
            for (lo, hi), entering, later in zip(ranges, lows, carries):
                span = slice(lo, hi)
                solved = part[z, span] + prodr[z, span] * entering + ratio[z, span] * later
                after = keep[z, span] * solved + source[z, span]
                state[z, span] = after
                if lo == 0:
                    edge[step, 0, z] = after[0:1]
                if hi == slab:
                    edge[step, 1, z] = after[hi - lo - 1:hi - lo]
                done.append(solved)
            return tuple(done)

        lax.fori_loop(0, m, body, tuple(highs), unroll=8)

    xs_wait(STEPS)
    lax.fori_loop(0, m, fix_body, 0, unroll=8)
    combine_coefficients()
    conc_load.wait()

    for step in range(STEPS):
        order = (1, 0) if step == 0 else (0, 1)
        for group in order:
            if group == 1:
                xs_wait(step)
            forward(step, spans[group])
            pair_v_copy(step, group).start()
            if step > 0:
                combine(step, group)
        if step == 0:
            for group in order:
                combine(step, group)
            prod_load.wait()
            lax.fori_loop(0, m, cell_body, 0, unroll=8)
            gather_coefficients()
        for group in order:
            if step == 0 or group == 0:
                interfaces(step, group)
            if step > 0 and group == 0:
                interfaces(step, 1)
            back_copy(step, group, False).wait_recv()
            backward(step, spans[group])
            if group == 1 and step < STEPS - 1:
                xs_start(step + 1, [edge.at[step, at, :, 0] for at in range(2)])

    for at in range(2):
        @pl.when(sides[at][0])
        def _(at=at):
            for slot in range(STEPS + 1):
                xs_copy(slot, at).wait_send()

        @pl.when(has_outer)
        def _(at=at):
            ax_copy(at).wait_send()

    face_copy().wait_send()

    to_peers(3, lambda count, to: coef_copy(count, chip, to).wait_send())

    def finish(group):
        pair_c_copy(group).wait_send()
        to_peers(2, lambda count, to: raw_copy(count, group, chip, to).wait_send())
        for step in range(STEPS):
            pair_v_copy(step, group).wait_send()
            back_copy(step, group, True).wait_send()
            if step > 0:
                for to in peers:
                    fold_copy(step, group, chip, to).wait_send()

    loop_groups(finish)


def on_device(n_ax, n_xs, conc, mask, layer, stiff, prod, diff_tab, upt_tab):
    m, slab, cols = conc.shape
    chips = n_ax // 2
    half, q = slab // 2, slab // 4
    f32 = jnp.float32
    cells = pltpu.VMEM((m, slab, cols), f32)
    labels = pltpu.VMEM((m, slab, cols), jnp.int32)
    dma = pltpu.SemaphoreType.DMA
    vmem = lambda *shape: pltpu.VMEM(shape, f32)
    hbm_spec = pl.BlockSpec(memory_space=pltpu.HBM)
    return pl.pallas_call(
        functools.partial(kernel, n_ax, n_xs),
        out_shape=pltpu.VMEM((m, slab, cols), f32),
        in_specs=[hbm_spec] * 7,
        out_specs=pl.BlockSpec(memory_space=pltpu.VMEM),
        scratch_shapes=[
            pltpu.SMEM(diff_tab.shape, f32), pltpu.SMEM(upt_tab.shape, f32),
            pltpu.VMEM((2, slab, cols), jnp.int32), pltpu.VMEM((2, slab, cols), jnp.int32),
            vmem(2, slab, cols), vmem(2, slab, cols),
            pltpu.VMEM((2, m, cols), jnp.int32), pltpu.VMEM((2, m, cols), jnp.int32),
            vmem(2, m, cols), vmem(2, m, cols),
            labels, labels, cells, cells, vmem(m + 1, slab, cols),
            cells, cells, cells, cells, cells, cells, cells, cells, cells, cells,
            vmem(STEPS, 2, m, 1, cols), vmem(STEPS + 1, 2, m, 1, cols),
            vmem(2, half, cols), vmem(2, half, cols),
            vmem(3, slab, cols), vmem(3, half, cols), vmem(chips, 3, half, cols),
            vmem(5, half, cols), vmem(chips, half, cols), vmem(chips, half, cols), vmem(chips + 1, half, cols),
            vmem(STEPS, 2, slab, cols), vmem(STEPS, 2, half, cols),
            vmem(chips, 2, 2, q, cols), vmem(STEPS, chips, 2, q, cols), vmem(STEPS, 2, 2, q, cols),
            vmem(3, half, cols), vmem(2, q, cols),
            vmem(STEPS, 2, slab, cols), vmem(STEPS, 2, 2, q, cols),
            dma((16 + 3 * LOADS,)), dma((STEPS + 1, 2)), dma((STEPS + 1, 2)), dma((2,)), dma((2,)), dma((2,)),
            dma((2,)), dma((2,)), dma((STEPS, 2)), dma((STEPS, 2)), dma((STEPS, 2)), dma((STEPS, 2)),
            dma((chips,)), dma((chips,)), dma((STEPS, 2, chips)), dma((STEPS, 2, chips)),
        ],
        compiler_params=pltpu.CompilerParams(
            collective_id=0, has_side_effects=True, vmem_limit_bytes=56 * 1024 * 1024
        ),
    )(conc, mask, layer, stiff, prod, diff_tab, upt_tab)


def solution(mesh):
    cells = P("ax", "xs", None)
    return jax.shard_map(
        functools.partial(on_device, mesh.shape["ax"], mesh.shape["xs"]),
        mesh=mesh, in_specs=(cells,) * 5 + (P(), P()), out_specs=cells, check_vma=False,
    )
```

```python
import functools

import jax
import jax.numpy as jnp
from jax import lax
from jax.experimental import pallas as pl
from jax.experimental.pallas import tpu as pltpu
from jax.sharding import PartitionSpec as P

STEPS = 2
RZ = 3072
SECTION_RATE = 0.05
LOADS = 4
AHEAD = 4
GREET = 1
CONC_AT = 1
PROD_AT = 2
MESH = pl.DeviceIdType.MESH


def lookup(labels, table):
    found = jnp.full(labels.shape, table[0], jnp.float32)
    for index in range(1, len(table)):
        found = jnp.where(labels == index, table[index], found)
    return found


def kernel(
    n_ax, n_xs,
    conc_hbm, mask_hbm, layer_hbm, stiff_hbm, prod_hbm, diff_hbm, upt_hbm,
    state,
    diff_tab, upt_tab,
    mask_face, layer_face, stiff_face, face, mask_rim, layer_rim, stiff_rim, rim, mask, layer, stiff, source, root, ratio, recip, prodr, part, w_lower, w_upper, w_left, w_right, centre, keep,
    edge, halo, beyond, mate_face, dev_c, pair_c, chip_c, links, gain_up, gain_down, face_gain,
    dev_v, pair_v, raw_v, fold_v, fold_out, found, heard, flow, back_out,
    in_sem, xs_send, xs_recv, ax_send, ax_recv, face_sem,
    pc_send, pc_recv, pv_send, pv_recv, bk_send, bk_recv, cc_send, cc_recv, cv_send, cv_recv,
):
    m, slab, cols = conc_hbm.shape
    chips = n_ax // 2
    half = slab // 2
    q = slab // 4
    f32 = jnp.float32
    me = lax.axis_index("ax")
    mx = lax.axis_index("xs")
    chip = lax.div(me, 2)
    core = lax.rem(me, 2)
    low = core == 0
    mate = {"ax": me + 1 - 2 * core}

    inside, ends = ((q, half + q),), ((0, q), (half + q, slab))

    def lines(mine, group):
        inner = jnp.where(low, q, half) if mine else jnp.where(low, half, q)
        outer = jnp.where(low, 0, half + q) if mine else jnp.where(low, half + q, 0)
        return pl.ds(pl.multiple_of(jnp.where(group == 0, inner, outer), 8), q)

    spans = (inside, ends)

    def halfway(group):
        return pl.ds(pl.multiple_of(jnp.where(low == (group == 0), q, 0), 8), q)

    def kept(group):
        return pl.ds(pl.multiple_of(group * q, 8), q)

    def local(src, dst, at):
        return pltpu.make_async_copy(src, dst, in_sem.at[at])

    chunk = m // LOADS
    arrays = [
        (mask_hbm, mask, mask_face, mask_rim), (layer_hbm, layer, layer_face, layer_rim),
        (stiff_hbm, stiff, stiff_face, stiff_rim),
    ]
    tables = [local(diff_hbm, diff_tab, 0), local(upt_hbm, upt_tab, 1)]
    face_loads = [
        local(src.at[z], dst.at[k], 2 + 2 * at + k)
        for at, (src, _, dst, _) in enumerate(arrays) for k, z in enumerate((0, m - 1))
    ]
    rim_loads = [
        local(src.at[:, line], dst.at[k], 8 + 2 * at + k)
        for at, (src, _, _, dst) in enumerate(arrays) for k, line in enumerate((0, slab - 1))
    ]
    conc_load = local(conc_hbm, state, 14)
    prod_load = local(prod_hbm, source, 15)

    def part_loads(at):
        planes = pl.ds(at * chunk, chunk)
        return [
            local(src.at[planes], dst.at[planes], 16 + 3 * at + k) for k, (src, dst, _, _) in enumerate(arrays)
        ]

    sides = (
        (mx > 0, {"xs": mx - 1}),
        (mx < n_xs - 1, {"xs": mx + 1}),
        (me > 0, {"ax": me - 1}),
        (me < n_ax - 1, {"ax": me + 1}),
    )
    last_chip = chip == chips - 1
    between = (chip > 0) & (chip < chips - 1)
    peers = [lax.rem(chip + reach, chips) for reach in range(chips - 1, 0, -1)]
    greeted = list(sides) + [(True, {"ax": 2 * to + core}) for to in peers]
    barrier = pltpu.get_barrier_semaphore()
    for there, peer in greeted:
        @pl.when(there)
        def _(peer=peer):
            pl.semaphore_signal(barrier, inc=1, device_id=peer, device_id_type=MESH)

    for load in tables + part_loads(0) + face_loads + rim_loads:
        load.start()
    for at in range(1, AHEAD):
        for load in part_loads(at):
            load.start()

    for at in range(2):
        @pl.when(jnp.logical_not(sides[at][0]))
        def _(at=at):
            for slot in range(STEPS + 1):
                halo[slot, at] = jnp.zeros((m, 1, cols), f32)

        @pl.when((chip == 0) if at == 0 else (chip == chips - 1))
        def _(at=at):
            beyond[at] = jnp.zeros((half, cols), f32)

    root[m] = jnp.zeros((slab, cols), f32)

    def xs_copy(slot, at, src=None):
        return pltpu.make_async_remote_copy(
            src_ref=rim.at[at] if src is None else src, dst_ref=halo.at[slot, 1 - at, :, 0],
            send_sem=xs_send.at[slot, at], recv_sem=xs_recv.at[slot, 1 - at],
            device_id=sides[at][1], device_id_type=MESH,
        )

    def xs_start(slot, sources):
        for at in range(2):
            @pl.when(sides[at][0])
            def _(at=at):
                xs_copy(slot, at, sources[at]).start()

    def xs_wait(slot):
        for at in range(2):
            @pl.when(sides[at][0])
            def _(at=at):
                xs_copy(slot, 1 - at).wait_recv()

    def ax_copy(to):
        step_to = jnp.where(low, -1, 1)
        return pltpu.make_async_remote_copy(
            src_ref=face.at[core, pl.ds(to * half, half)], dst_ref=beyond.at[1 - core],
            send_sem=ax_send.at[to], recv_sem=ax_recv.at[1 - core],
            device_id={"ax": 2 * (chip + step_to) + to}, device_id_type=MESH,
        )

    def ax_landed(at):
        return pltpu.make_async_remote_copy(
            src_ref=face.at[0, pl.ds(0, half)], dst_ref=beyond.at[at],
            send_sem=ax_send.at[0], recv_sem=ax_recv.at[at], device_id=mate, device_id_type=MESH,
        )

    def face_copy():
        return pltpu.make_async_remote_copy(
            src_ref=face.at[:, pl.ds(pl.multiple_of((1 - core) * half, 8), half)], dst_ref=mate_face,
            send_sem=face_sem.at[0], recv_sem=face_sem.at[1], device_id=mate, device_id_type=MESH,
        )

    has_outer = jnp.where(low, chip > 0, chip < chips - 1)

    for load in tables:
        load.wait()
    scaled_table = [RZ * diff_tab[index] for index in range(diff_tab.shape[0])]

    def scaled_root(mask_now, layer_now, stiff_now):
        square = lookup(layer_now, scaled_table) * stiff_now
        return jnp.where(mask_now != 0, square * lax.rsqrt(square), 0.0)

    row_at = lax.broadcasted_iota(jnp.int32, (slab, cols), 0)
    col_at = lax.broadcasted_iota(jnp.int32, (slab, cols), 1)

    def root_part(at, carry):
        @pl.when(at == GREET)
        def _():
            for load in face_loads + rim_loads:
                load.wait()
            for end in range(2):
                face[end] = scaled_root(mask_face[end], layer_face[end], stiff_face[end])
                rim[end] = scaled_root(mask_rim[end], layer_rim[end], stiff_rim[end])
            pl.semaphore_wait(barrier, sum(jnp.where(there, 1, 0) for there, _ in greeted))
            @pl.when(has_outer)
            def _():
                for to in range(2):
                    ax_copy(to).start()

            face_copy().start()
            xs_start(STEPS, [rim.at[0], rim.at[1]])
            xs_start(0, [conc_hbm.at[:, 0], conc_hbm.at[:, slab - 1]])

        for load in part_loads(at):
            load.wait()

        if AHEAD < LOADS:
            @pl.when(at + AHEAD < LOADS)
            def _():
                for load in part_loads(at + AHEAD):
                    load.start()

        @pl.when(at == CONC_AT)
        def _():
            conc_load.start()

        @pl.when(at == PROD_AT)
        def _():
            prod_load.start()

        for offset in range(chunk):
            z = at * chunk + offset
            value = scaled_root(mask[z], layer[z], stiff[z])
            root[z] = value
        return carry

    lax.fori_loop(0, LOADS, root_part, 0)

    def factor_body(z, carry):
        excess, product, total = carry
        band = root[z] * root[z + 1]
        inverse = pl.reciprocal(excess + band, approx=True)
        ratio_now = band * inverse
        scaled = product * inverse
        ratio[z] = ratio_now
        recip[z] = inverse
        prodr[z] = scaled
        return 1.0 + ratio_now * excess, product * ratio_now, total + product * scaled

    ones = jnp.ones((slab, cols), f32)
    _, _, total = lax.fori_loop(0, m, factor_body, (ones, ones, 0.0 * ones), unroll=8)
    sigma = recip[m - 1]
    ratio[m - 1] = sigma

    dev_c[0] = total
    dev_c[1] = prodr[m - 1]
    dev_c[2] = sigma

    def weight_body(z, carry):
        value = root[z]
        scaled = (SECTION_RATE / RZ) * value
        to_lower = jnp.where(row_at == 0, 0.0, scaled * pltpu.roll(value, 1, 0))
        to_left = jnp.where(col_at == 0, 0.0, scaled * pltpu.roll(value, 1, 1))
        to_upper = pltpu.roll(to_lower, slab - 1, 0)
        to_right = pltpu.roll(to_left, cols - 1, 1)
        w_lower[z], w_upper[z], w_left[z], w_right[z] = to_lower, to_upper, to_left, to_right
        centre[z] = 1.0 - ((to_lower + to_upper) + (to_left + to_right))
        return carry

    def mate_copy(src, dst, send, recv):
        return pltpu.make_async_remote_copy(
            src_ref=src, dst_ref=dst, send_sem=send, recv_sem=recv, device_id=mate, device_id_type=MESH
        )

    def pair_c_copy(group):
        return mate_copy(
            dev_c.at[:, lines(False, group)], pair_c.at[:, kept(group)], pc_send.at[group], pc_recv.at[group]
        )

    def pair_v_copy(step, group):
        return mate_copy(
            dev_v.at[step, :, lines(False, group)], pair_v.at[step, :, kept(group)],
            pv_send.at[step, group], pv_recv.at[step, group],
        )

    def back_copy(step, group, mine):
        return mate_copy(
            back_out.at[step, group], flow.at[step, :, lines(mine, group)],
            bk_send.at[step, group], bk_recv.at[step, group],
        )

    def far_copy(src, dst, send, recv, to):
        return pltpu.make_async_remote_copy(
            src_ref=src, dst_ref=dst, send_sem=send, recv_sem=recv,
            device_id={"ax": 2 * to + core}, device_id_type=MESH,
        )

    def coef_copy(count, sender, to):
        rows = pl.ds(3 - count, count)
        return far_copy(
            chip_c.at[chip, rows], chip_c.at[sender, rows], cc_send.at[to], cc_recv.at[sender], to
        )

    def raw_copy(count, group, sender, to):
        rows = pl.ds(2 - count, count)
        return far_copy(
            raw_v.at[chip, group, rows], raw_v.at[sender, group, rows],
            cv_send.at[0, group, to], cv_recv.at[0, group, sender], to,
        )

    def fold_copy(step, group, sender, to):
        return far_copy(
            fold_out.at[step, group, jnp.where(to > chip, 1, 0)], fold_v.at[step, sender, group],
            cv_send.at[step, group, to], cv_recv.at[step, group, sender], to,
        )

    def to_peers(count, act):
        @pl.when(between)
        def _():
            for to in peers:
                act(count, to)

        @pl.when(jnp.logical_not(between))
        def _():
            for to in peers:
                act(1, to)

    def from_peers(count, act):
        for sender in range(chips):
            @pl.when(chip != sender)
            def _(sender=sender):
                act(count if 0 < sender < chips - 1 else 1, sender)

    def tau_of(at):
        return chip_c[at, 2 if at == chips - 1 else 1]

    def sigma_of(at):
        return chip_c[at, 1 if at == chips - 1 else 2]

    def loop_groups(act):
        def body(group, carry):
            act(group)
            return carry

        lax.fori_loop(0, 2, body, 0)

    loop_groups(lambda group: pair_c_copy(group).start())
    lax.fori_loop(0, m, weight_body, 0, unroll=8)

    def combine_coefficients():
        def one(group):
            pair_c_copy(group).wait_recv()
            at = kept(group)
            mine = [dev_c[row, lines(True, group)] for row in range(3)]
            his = [pair_c[row, at] for row in range(3)]
            tau_l, rho_l, sigma_l = [jnp.where(low, a, b) for a, b in zip(mine, his)]
            tau_u, rho_u, sigma_u = [jnp.where(low, b, a) for a, b in zip(mine, his)]
            near = halfway(group)
            face_l, face_u = [
                [jnp.where(low == lower, face[k, lines(True, group)], mate_face[k, near]) for k in range(2)]
                for lower in (True, False)
            ]
            band = face_l[1] * face_u[0]
            joint = band * pl.reciprocal(1.0 + band * (sigma_l + tau_u), approx=True)
            link_l, link_u = rho_l * joint, rho_u * joint
            band_low, band_high = beyond[0, near] * face_l[0], face_u[1] * beyond[1, near]
            scale_low, scale_high = jnp.sqrt(band_low), jnp.sqrt(band_high)
            links[0, at], links[1, at], links[2, at] = joint, link_l, link_u
            links[3, at], links[4, at] = scale_low, scale_high
            tau, sigma = band_low * (tau_l - rho_l * link_l), band_high * (sigma_u - rho_u * link_u)
            chip_c[chip, 0, at] = (scale_low * scale_high) * (rho_l * link_u)
            chip_c[chip, 1, at] = jnp.where(last_chip, sigma, tau)
            chip_c[chip, 2, at] = jnp.where(last_chip, tau, sigma)

        for at in range(2):
            @pl.when((chip > 0) if at == 0 else (chip < chips - 1))
            def _(at=at):
                ax_landed(at).wait_recv()

        face_copy().wait_recv()
        loop_groups(one)
        to_peers(3, lambda count, to: coef_copy(count, chip, to).start())

    def gather_coefficients():
        from_peers(3, lambda count, sender: coef_copy(count, sender, sender).wait_recv())
        zero = jnp.zeros((half, cols), f32)
        below, above = [zero] * (chips + 1), [zero] * (chips + 1)
        gain_up[0] = zero
        gain_up[chips - 1] = zero
        gain_down[0] = zero
        gain_down[chips - 1] = zero
        below[1] = sigma_of(0)
        for at in range(1, chips - 1):
            gain = chip_c[at, 0] * pl.reciprocal(1.0 + below[at] + tau_of(at), approx=True)
            gain_up[at] = gain
            below[at + 1] = sigma_of(at) - gain * chip_c[at, 0]
        above[chips - 1] = tau_of(chips - 1)
        for at in range(chips - 2, 0, -1):
            gain = chip_c[at, 0] * pl.reciprocal(1.0 + above[at + 1] + sigma_of(at), approx=True)
            gain_down[at] = gain
            above[at] = tau_of(at) - gain * chip_c[at, 0]
        face_gain[0] = zero
        face_gain[chips] = zero
        for at in range(1, chips):
            face_gain[at] = pl.reciprocal(1.0 + below[at] + above[at], approx=True)

    def fix_body(z, carry):
        first, last = slice(0, 1), slice(slab - 1, slab)
        to_lower = (SECTION_RATE / RZ) * root[z, first] * halo[STEPS, 0, z]
        to_upper = (SECTION_RATE / RZ) * root[z, last] * halo[STEPS, 1, z]
        w_lower[z, first] = to_lower
        w_upper[z, last] = to_upper
        centre[z, first] = centre[z, first] - to_lower
        centre[z, last] = centre[z, last] - to_upper
        return carry

    keep_table = [1.0 - upt_tab[index] for index in range(upt_tab.shape[0])]

    def cell_body(z, carry):
        there = mask[z] != 0
        keep[z] = jnp.where(there, lookup(layer[z], keep_table), 1.0)
        source[z] = jnp.where(there, source[z], 0.0)
        return carry

    def forward(step, ranges):
        def body(z, carries):
            done = []
            for (lo, hi), (moved, first) in zip(ranges, carries):
                span = slice(lo, hi)
                size = hi - lo
                row = lax.broadcasted_iota(jnp.int32, (size, cols), 0)
                now = state[z, span]
                before = halo[step, 0, z] if lo == 0 else state[z, lo - 1:lo]
                behind = halo[step, 1, z] if hi == slab else state[z, hi:hi + 1]
                lower = jnp.where(row == 0, before, pltpu.roll(now, 1, 0))
                upper = jnp.where(row == size - 1, behind, pltpu.roll(now, size - 1, 0))
                across = w_left[z, span] * pltpu.roll(now, 1, 1) + w_right[z, span] * pltpu.roll(now, cols - 1, 1)
                along = w_lower[z, span] * lower + w_upper[z, span] * upper
                explicit = (centre[z, span] * now + along) + across
                value = explicit + moved
                part[z, span] = recip[z, span] * value
                done.append((ratio[z, span] * value, first + prodr[z, span] * value))
            return tuple(done)

        zeros = [jnp.zeros((hi - lo, cols), f32) for lo, hi in ranges]
        sums = lax.fori_loop(0, m, body, tuple((zero, zero) for zero in zeros), unroll=16)
        for (lo, hi), (_, first) in zip(ranges, sums):
            span = slice(lo, hi)
            dev_v[step, 0, span] = first
            dev_v[step, 1, span] = part[m - 1, span]

    def forward_mate_first(step, group):
        lower, upper = ((q, half), (half, half + q)) if group == 0 else ((0, q), (half + q, slab))

        def run(first, second):
            forward(step, (first,))
            pair_v_copy(step, group).start()
            forward(step, (second,))

        pl.when(low)(lambda: run(upper, lower))
        pl.when(jnp.logical_not(low))(lambda: run(lower, upper))

    def combine(step, group):
        at = kept(group)
        pair_v_copy(step, group).wait_recv()
        mine = [dev_v[step, row, lines(True, group)] for row in range(2)]
        his = [pair_v[step, row, at] for row in range(2)]
        first_l, last_l = [jnp.where(low, a, b) for a, b in zip(mine, his)]
        first_u, last_u = [jnp.where(low, b, a) for a, b in zip(mine, his)]
        gap = last_l - first_u
        first = links[3, at] * (first_l - links[1, at] * gap)
        last = links[4, at] * (last_u + links[2, at] * gap)
        found[0, at], found[1, at], found[2, at] = links[0, at] * gap, first, last

        if step == 0:
            raw_v[chip, group, 0] = jnp.where(last_chip, last, first)
            raw_v[chip, group, 1] = jnp.where(last_chip, first, last)
            to_peers(2, lambda count, to: raw_copy(count, group, chip, to).start())

        if step > 0:
            fold_out[step, group, 0] = first - gain_down[chip, at] * last
            fold_out[step, group, 1] = last - gain_up[chip, at] * first
            for to in peers:
                fold_copy(step, group, chip, to).start()

    def interfaces(step, group):
        at = kept(group)

        if step == 0:
            from_peers(2, lambda count, sender: raw_copy(count, group, sender, sender).wait_recv())
            below = jnp.zeros((q, cols), f32)
            above = jnp.zeros((q, cols), f32)
            for sender in range(chips - 1):
                there = raw_v[sender, group, 1]
                if sender > 0:
                    there = there + gain_up[sender, at] * (below - raw_v[sender, group, 0])
                below = jnp.where(sender < chip, there, below)
            for sender in range(chips - 1, 0, -1):
                if sender == chips - 1:
                    there = raw_v[sender, group, 1]
                else:
                    there = raw_v[sender, group, 0] - gain_down[sender, at] * (raw_v[sender, group, 1] - above)
                above = jnp.where(sender > chip, there, above)
            heard[0], heard[1] = below, above

        if step > 0:
            for sender in peers:
                fold_copy(step, group, sender, sender).wait_recv()
            below = jnp.zeros((q, cols), f32)
            above = jnp.zeros((q, cols), f32)
            for sender in range(chips - 1):
                there = fold_v[step, sender, group] + gain_up[sender, at] * below
                below = jnp.where(sender < chip, there, below)
            for sender in range(chips - 1, 0, -1):
                there = fold_v[step, sender, group] + gain_down[sender, at] * above
                above = jnp.where(sender > chip, there, above)
            heard[0], heard[1] = below, above

        below, above = heard[0], heard[1]
        gap, first, last = found[0, at], found[1, at], found[2, at]
        from_low = last + gain_up[chip, at] * (below - first)
        from_high = first - gain_down[chip, at] * (last - above)
        flow_low = (below - from_high) * face_gain[chip, at] * links[3, at]
        flow_high = (from_low - above) * face_gain[chip + 1, at] * links[4, at]
        flow_mid = gap + links[1, at] * flow_low + links[2, at] * flow_high
        flow[step, 0, lines(True, group)] = flow_mid
        flow[step, 1, lines(True, group)] = jnp.where(low, flow_low, flow_high)
        back_out[step, group, 0] = flow_mid
        back_out[step, group, 1] = jnp.where(low, flow_high, flow_low)
        back_copy(step, group, True).start()

    def backward(step, ranges):
        lows = []
        highs = []
        for lo, hi in ranges:
            span = slice(lo, hi)
            mid, outer = flow[step, 0, span], flow[step, 1, span]
            lows.append(jnp.where(low, outer, mid))
            highs.append(-jnp.where(low, mid, outer))

        def body(at, carries):
            z = m - 1 - at
            done = []
            for (lo, hi), entering, later in zip(ranges, lows, carries):
                span = slice(lo, hi)
                solved = part[z, span] + prodr[z, span] * entering + ratio[z, span] * later
                after = keep[z, span] * solved + source[z, span]
                state[z, span] = after
                if lo == 0:
                    edge[step, 0, z] = after[0:1]
                if hi == slab:
                    edge[step, 1, z] = after[hi - lo - 1:hi - lo]
                done.append(solved)
            return tuple(done)

        lax.fori_loop(0, m, body, tuple(highs), unroll=8)

    combine_coefficients()
    xs_wait(STEPS)
    lax.fori_loop(0, m, fix_body, 0, unroll=8)
    conc_load.wait()

    for step in range(STEPS):
        order = (1, 0) if step == 0 else (0, 1)
        for group in order:
            if group == 1:
                xs_wait(step)
            if step == STEPS - 1 and group == 1:
                forward_mate_first(step, group)
            else:
                forward(step, spans[group])
                pair_v_copy(step, group).start()
            if step > 0:
                combine(step, group)
        if step == 0:
            for group in order:
                combine(step, group)
            prod_load.wait()
            lax.fori_loop(0, m, cell_body, 0, unroll=8)
            gather_coefficients()
        for group in order:
            if step == 0 or group == 0:
                interfaces(step, group)
            if step > 0 and group == 0:
                interfaces(step, 1)
            back_copy(step, group, False).wait_recv()
            backward(step, spans[group])
            if group == 1 and step < STEPS - 1:
                xs_start(step + 1, [edge.at[step, at, :, 0] for at in range(2)])

    for at in range(2):
        @pl.when(sides[at][0])
        def _(at=at):
            for slot in range(STEPS + 1):
                xs_copy(slot, at).wait_send()

        @pl.when(has_outer)
        def _(at=at):
            ax_copy(at).wait_send()

    face_copy().wait_send()

    to_peers(3, lambda count, to: coef_copy(count, chip, to).wait_send())

    def finish(group):
        pair_c_copy(group).wait_send()
        to_peers(2, lambda count, to: raw_copy(count, group, chip, to).wait_send())
        for step in range(STEPS):
            pair_v_copy(step, group).wait_send()
            back_copy(step, group, True).wait_send()
            if step > 0:
                for to in peers:
                    fold_copy(step, group, chip, to).wait_send()

    loop_groups(finish)


def on_device(n_ax, n_xs, conc, mask, layer, stiff, prod, diff_tab, upt_tab):
    m, slab, cols = conc.shape
    chips = n_ax // 2
    half, q = slab // 2, slab // 4
    f32 = jnp.float32
    cells = pltpu.VMEM((m, slab, cols), f32)
    labels = pltpu.VMEM((m, slab, cols), jnp.int32)
    dma = pltpu.SemaphoreType.DMA
    vmem = lambda *shape: pltpu.VMEM(shape, f32)
    hbm_spec = pl.BlockSpec(memory_space=pltpu.HBM)
    return pl.pallas_call(
        functools.partial(kernel, n_ax, n_xs),
        out_shape=pltpu.VMEM((m, slab, cols), f32),
        in_specs=[hbm_spec] * 7,
        out_specs=pl.BlockSpec(memory_space=pltpu.VMEM),
        scratch_shapes=[
            pltpu.SMEM(diff_tab.shape, f32), pltpu.SMEM(upt_tab.shape, f32),
            pltpu.VMEM((2, slab, cols), jnp.int32), pltpu.VMEM((2, slab, cols), jnp.int32),
            vmem(2, slab, cols), vmem(2, slab, cols),
            pltpu.VMEM((2, m, cols), jnp.int32), pltpu.VMEM((2, m, cols), jnp.int32),
            vmem(2, m, cols), vmem(2, m, cols),
            labels, labels, cells, cells, vmem(m + 1, slab, cols),
            cells, cells, cells, cells, cells, cells, cells, cells, cells, cells,
            vmem(STEPS, 2, m, 1, cols), vmem(STEPS + 1, 2, m, 1, cols),
            vmem(2, half, cols), vmem(2, half, cols),
            vmem(3, slab, cols), vmem(3, half, cols), vmem(chips, 3, half, cols),
            vmem(5, half, cols), vmem(chips, half, cols), vmem(chips, half, cols), vmem(chips + 1, half, cols),
            vmem(STEPS, 2, slab, cols), vmem(STEPS, 2, half, cols),
            vmem(chips, 2, 2, q, cols), vmem(STEPS, chips, 2, q, cols), vmem(STEPS, 2, 2, q, cols),
            vmem(3, half, cols), vmem(2, q, cols),
            vmem(STEPS, 2, slab, cols), vmem(STEPS, 2, 2, q, cols),
            dma((16 + 3 * LOADS,)), dma((STEPS + 1, 2)), dma((STEPS + 1, 2)), dma((2,)), dma((2,)), dma((2,)),
            dma((2,)), dma((2,)), dma((STEPS, 2)), dma((STEPS, 2)), dma((STEPS, 2)), dma((STEPS, 2)),
            dma((chips,)), dma((chips,)), dma((STEPS, 2, chips)), dma((STEPS, 2, chips)),
        ],
        compiler_params=pltpu.CompilerParams(
            collective_id=0, has_side_effects=True, vmem_limit_bytes=56 * 1024 * 1024
        ),
    )(conc, mask, layer, stiff, prod, diff_tab, upt_tab)


def solution(mesh):
    cells = P("ax", "xs", None)
    return jax.shard_map(
        functools.partial(on_device, mesh.shape["ax"], mesh.shape["xs"]),
        mesh=mesh, in_specs=(cells,) * 5 + (P(), P()), out_specs=cells, check_vma=False,
    )
```

```python
import functools

import jax
import jax.numpy as jnp
from jax import lax
from jax.experimental import pallas as pl
from jax.experimental.pallas import tpu as pltpu
from jax.sharding import PartitionSpec as P

STEPS = 2
RZ = 3072
SECTION_RATE = 0.05
LOADS = 4
AHEAD = 4
GREET = 1
CONC_AT = 1
PROD_AT = 2
MESH = pl.DeviceIdType.MESH


def lookup(labels, table):
    found = jnp.full(labels.shape, table[0], jnp.float32)
    for index in range(1, len(table)):
        found = jnp.where(labels == index, table[index], found)
    return found


def kernel(
    n_ax, n_xs,
    conc_hbm, mask_hbm, layer_hbm, stiff_hbm, prod_hbm, diff_hbm, upt_hbm,
    state,
    diff_tab, upt_tab,
    mask_face, layer_face, stiff_face, face, mask_rim, layer_rim, stiff_rim, rim, mask, layer, stiff, source, root, ratio, recip, prodr, part, w_lower, w_upper, w_left, w_right, centre, keep,
    edge, halo, beyond, mate_face, dev_c, pair_c, chip_c, links, gain_up, gain_down, face_gain,
    dev_v, pair_v, raw_v, fold_v, fold_out, found, heard, flow, back_out,
    in_sem, xs_send, xs_recv, ax_send, ax_recv, face_sem,
    pc_send, pc_recv, pv_send, pv_recv, bk_send, bk_recv, cc_send, cc_recv, cv_send, cv_recv,
):
    m, slab, cols = conc_hbm.shape
    chips = n_ax // 2
    half = slab // 2
    q = slab // 4
    f32 = jnp.float32
    me = lax.axis_index("ax")
    mx = lax.axis_index("xs")
    chip = lax.div(me, 2)
    core = lax.rem(me, 2)
    low = core == 0
    mate = {"ax": me + 1 - 2 * core}

    inside, ends = ((q, half + q),), ((0, q), (half + q, slab))

    def lines(mine, group):
        inner = jnp.where(low, q, half) if mine else jnp.where(low, half, q)
        outer = jnp.where(low, 0, half + q) if mine else jnp.where(low, half + q, 0)
        return pl.ds(pl.multiple_of(jnp.where(group == 0, inner, outer), 8), q)

    spans = (inside, ends)

    def halfway(group):
        return pl.ds(pl.multiple_of(jnp.where(low == (group == 0), q, 0), 8), q)

    def kept(group):
        return pl.ds(pl.multiple_of(group * q, 8), q)

    def local(src, dst, at):
        return pltpu.make_async_copy(src, dst, in_sem.at[at])

    chunk = m // LOADS
    arrays = [
        (mask_hbm, mask, mask_face, mask_rim), (layer_hbm, layer, layer_face, layer_rim),
        (stiff_hbm, stiff, stiff_face, stiff_rim),
    ]
    tables = [local(diff_hbm, diff_tab, 0), local(upt_hbm, upt_tab, 1)]
    face_loads = [
        local(src.at[z], dst.at[k], 2 + 2 * at + k)
        for at, (src, _, dst, _) in enumerate(arrays) for k, z in enumerate((0, m - 1))
    ]
    rim_loads = [
        local(src.at[:, line], dst.at[k], 8 + 2 * at + k)
        for at, (src, _, _, dst) in enumerate(arrays) for k, line in enumerate((0, slab - 1))
    ]
    conc_load = local(conc_hbm, state, 14)
    prod_load = local(prod_hbm, source, 15)

    def part_loads(at):
        planes = pl.ds(at * chunk, chunk)
        return [
            local(src.at[planes], dst.at[planes], 16 + 3 * at + k) for k, (src, dst, _, _) in enumerate(arrays)
        ]

    sides = (
        (mx > 0, {"xs": mx - 1}),
        (mx < n_xs - 1, {"xs": mx + 1}),
        (me > 0, {"ax": me - 1}),
        (me < n_ax - 1, {"ax": me + 1}),
    )
    last_chip = chip == chips - 1
    between = (chip > 0) & (chip < chips - 1)
    peers = [lax.rem(chip + reach, chips) for reach in range(chips - 1, 0, -1)]
    greeted = list(sides) + [(True, {"ax": 2 * to + core}) for to in peers]
    barrier = pltpu.get_barrier_semaphore()
    for there, peer in greeted:
        @pl.when(there)
        def _(peer=peer):
            pl.semaphore_signal(barrier, inc=1, device_id=peer, device_id_type=MESH)

    for load in tables + part_loads(0) + face_loads + rim_loads:
        load.start()
    for at in range(1, AHEAD):
        for load in part_loads(at):
            load.start()

    for at in range(2):
        @pl.when(jnp.logical_not(sides[at][0]))
        def _(at=at):
            for slot in range(STEPS + 1):
                halo[slot, at] = jnp.zeros((m, 1, cols), f32)

        @pl.when((chip == 0) if at == 0 else (chip == chips - 1))
        def _(at=at):
            beyond[at] = jnp.zeros((half, cols), f32)

    root[m] = jnp.zeros((slab, cols), f32)

    def xs_copy(slot, at, src=None):
        return pltpu.make_async_remote_copy(
            src_ref=rim.at[at] if src is None else src, dst_ref=halo.at[slot, 1 - at, :, 0],
            send_sem=xs_send.at[slot, at], recv_sem=xs_recv.at[slot, 1 - at],
            device_id=sides[at][1], device_id_type=MESH,
        )

    def xs_start(slot, sources):
        for at in range(2):
            @pl.when(sides[at][0])
            def _(at=at):
                xs_copy(slot, at, sources[at]).start()

    def xs_wait(slot):
        for at in range(2):
            @pl.when(sides[at][0])
            def _(at=at):
                xs_copy(slot, 1 - at).wait_recv()

    def ax_copy(to):
        step_to = jnp.where(low, -1, 1)
        return pltpu.make_async_remote_copy(
            src_ref=face.at[core, pl.ds(to * half, half)], dst_ref=beyond.at[1 - core],
            send_sem=ax_send.at[to], recv_sem=ax_recv.at[1 - core],
            device_id={"ax": 2 * (chip + step_to) + to}, device_id_type=MESH,
        )

    def ax_landed(at):
        return pltpu.make_async_remote_copy(
            src_ref=face.at[0, pl.ds(0, half)], dst_ref=beyond.at[at],
            send_sem=ax_send.at[0], recv_sem=ax_recv.at[at], device_id=mate, device_id_type=MESH,
        )

    def face_copy():
        return pltpu.make_async_remote_copy(
            src_ref=face.at[:, pl.ds(pl.multiple_of((1 - core) * half, 8), half)], dst_ref=mate_face,
            send_sem=face_sem.at[0], recv_sem=face_sem.at[1], device_id=mate, device_id_type=MESH,
        )

    has_outer = jnp.where(low, chip > 0, chip < chips - 1)

    for load in tables:
        load.wait()
    scaled_table = [RZ * diff_tab[index] for index in range(diff_tab.shape[0])]

    def scaled_root(mask_now, layer_now, stiff_now):
        square = lookup(layer_now, scaled_table) * stiff_now
        return jnp.where(mask_now != 0, square * lax.rsqrt(square), 0.0)

    row_at = lax.broadcasted_iota(jnp.int32, (slab, cols), 0)
    col_at = lax.broadcasted_iota(jnp.int32, (slab, cols), 1)

    def root_part(at, carry):
        @pl.when(at == GREET)
        def _():
            for load in face_loads + rim_loads:
                load.wait()
            for end in range(2):
                face[end] = scaled_root(mask_face[end], layer_face[end], stiff_face[end])
                rim[end] = scaled_root(mask_rim[end], layer_rim[end], stiff_rim[end])
            pl.semaphore_wait(barrier, sum(jnp.where(there, 1, 0) for there, _ in greeted))
            @pl.when(has_outer)
            def _():
                for to in range(2):
                    ax_copy(to).start()

            face_copy().start()
            xs_start(STEPS, [rim.at[0], rim.at[1]])
            xs_start(0, [conc_hbm.at[:, 0], conc_hbm.at[:, slab - 1]])

        for load in part_loads(at):
            load.wait()

        if AHEAD < LOADS:
            @pl.when(at + AHEAD < LOADS)
            def _():
                for load in part_loads(at + AHEAD):
                    load.start()

        @pl.when(at == CONC_AT)
        def _():
            conc_load.start()

        @pl.when(at == PROD_AT)
        def _():
            prod_load.start()

        for offset in range(chunk):
            z = at * chunk + offset
            value = scaled_root(mask[z], layer[z], stiff[z])
            root[z] = value
        return carry

    lax.fori_loop(0, LOADS, root_part, 0)

    def factor_body(z, carry):
        excess, product, total = carry
        band = root[z] * root[z + 1]
        inverse = pl.reciprocal(excess + band, approx=True)
        ratio_now = band * inverse
        scaled = product * inverse
        ratio[z] = ratio_now
        recip[z] = inverse
        prodr[z] = scaled
        return 1.0 + ratio_now * excess, product * ratio_now, total + product * scaled

    ones = jnp.ones((slab, cols), f32)
    _, _, total = lax.fori_loop(0, m, factor_body, (ones, ones, 0.0 * ones), unroll=8)
    sigma = recip[m - 1]
    ratio[m - 1] = sigma

    dev_c[0] = total
    dev_c[1] = prodr[m - 1]
    dev_c[2] = sigma

    def weight_body(z, carry):
        value = root[z]
        scaled = (SECTION_RATE / RZ) * value
        to_lower = jnp.where(row_at == 0, 0.0, scaled * pltpu.roll(value, 1, 0))
        to_left = jnp.where(col_at == 0, 0.0, scaled * pltpu.roll(value, 1, 1))
        to_upper = pltpu.roll(to_lower, slab - 1, 0)
        to_right = pltpu.roll(to_left, cols - 1, 1)
        w_lower[z], w_upper[z], w_left[z], w_right[z] = to_lower, to_upper, to_left, to_right
        centre[z] = 1.0 - ((to_lower + to_upper) + (to_left + to_right))
        return carry

    def mate_copy(src, dst, send, recv):
        return pltpu.make_async_remote_copy(
            src_ref=src, dst_ref=dst, send_sem=send, recv_sem=recv, device_id=mate, device_id_type=MESH
        )

    def pair_c_copy(group):
        return mate_copy(
            dev_c.at[:, lines(False, group)], pair_c.at[:, kept(group)], pc_send.at[group], pc_recv.at[group]
        )

    def pair_v_copy(step, group):
        return mate_copy(
            dev_v.at[step, :, lines(False, group)], pair_v.at[step, :, kept(group)],
            pv_send.at[step, group], pv_recv.at[step, group],
        )

    def back_copy(step, group, mine):
        return mate_copy(
            back_out.at[step, group], flow.at[step, :, lines(mine, group)],
            bk_send.at[step, group], bk_recv.at[step, group],
        )

    def far_copy(src, dst, send, recv, to):
        return pltpu.make_async_remote_copy(
            src_ref=src, dst_ref=dst, send_sem=send, recv_sem=recv,
            device_id={"ax": 2 * to + core}, device_id_type=MESH,
        )

    def coef_copy(count, sender, to):
        rows = pl.ds(3 - count, count)
        return far_copy(
            chip_c.at[chip, rows], chip_c.at[sender, rows], cc_send.at[to], cc_recv.at[sender], to
        )

    def raw_copy(count, group, sender, to):
        rows = pl.ds(2 - count, count)
        return far_copy(
            raw_v.at[chip, group, rows], raw_v.at[sender, group, rows],
            cv_send.at[0, group, to], cv_recv.at[0, group, sender], to,
        )

    def fold_copy(step, group, sender, to):
        return far_copy(
            fold_out.at[step, group, jnp.where(to > chip, 1, 0)], fold_v.at[step, sender, group],
            cv_send.at[step, group, to], cv_recv.at[step, group, sender], to,
        )

    def to_peers(count, act):
        @pl.when(between)
        def _():
            for to in peers:
                act(count, to)

        @pl.when(jnp.logical_not(between))
        def _():
            for to in peers:
                act(1, to)

    def from_peers(count, act):
        for sender in range(chips):
            @pl.when(chip != sender)
            def _(sender=sender):
                act(count if 0 < sender < chips - 1 else 1, sender)

    def tau_of(at):
        return chip_c[at, 2 if at == chips - 1 else 1]

    def sigma_of(at):
        return chip_c[at, 1 if at == chips - 1 else 2]

    def loop_groups(act):
        def body(group, carry):
            act(group)
            return carry

        lax.fori_loop(0, 2, body, 0)

    loop_groups(lambda group: pair_c_copy(group).start())
    lax.fori_loop(0, m, weight_body, 0, unroll=8)

    def combine_coefficients():
        def one(group):
            pair_c_copy(group).wait_recv()
            at = kept(group)
            mine = [dev_c[row, lines(True, group)] for row in range(3)]
            his = [pair_c[row, at] for row in range(3)]
            tau_l, rho_l, sigma_l = [jnp.where(low, a, b) for a, b in zip(mine, his)]
            tau_u, rho_u, sigma_u = [jnp.where(low, b, a) for a, b in zip(mine, his)]
            near = halfway(group)
            face_l, face_u = [
                [jnp.where(low == lower, face[k, lines(True, group)], mate_face[k, near]) for k in range(2)]
                for lower in (True, False)
            ]
            band = face_l[1] * face_u[0]
            joint = band * pl.reciprocal(1.0 + band * (sigma_l + tau_u), approx=True)
            link_l, link_u = rho_l * joint, rho_u * joint
            band_low, band_high = beyond[0, near] * face_l[0], face_u[1] * beyond[1, near]
            scale_low, scale_high = jnp.sqrt(band_low), jnp.sqrt(band_high)
            links[0, at], links[1, at], links[2, at] = joint, link_l, link_u
            links[3, at], links[4, at] = scale_low, scale_high
            tau, sigma = band_low * (tau_l - rho_l * link_l), band_high * (sigma_u - rho_u * link_u)
            chip_c[chip, 0, at] = (scale_low * scale_high) * (rho_l * link_u)
            chip_c[chip, 1, at] = jnp.where(last_chip, sigma, tau)
            chip_c[chip, 2, at] = jnp.where(last_chip, tau, sigma)

        for at in range(2):
            @pl.when((chip > 0) if at == 0 else (chip < chips - 1))
            def _(at=at):
                ax_landed(at).wait_recv()

        face_copy().wait_recv()
        loop_groups(one)
        to_peers(3, lambda count, to: coef_copy(count, chip, to).start())

    def gather_coefficients():
        from_peers(3, lambda count, sender: coef_copy(count, sender, sender).wait_recv())
        zero = jnp.zeros((half, cols), f32)
        below, above = [zero] * (chips + 1), [zero] * (chips + 1)
        gain_up[0] = zero
        gain_up[chips - 1] = zero
        gain_down[0] = zero
        gain_down[chips - 1] = zero
        below[1] = sigma_of(0)
        for at in range(1, chips - 1):
            gain = chip_c[at, 0] * pl.reciprocal(1.0 + below[at] + tau_of(at), approx=True)
            gain_up[at] = gain
            below[at + 1] = sigma_of(at) - gain * chip_c[at, 0]
        above[chips - 1] = tau_of(chips - 1)
        for at in range(chips - 2, 0, -1):
            gain = chip_c[at, 0] * pl.reciprocal(1.0 + above[at + 1] + sigma_of(at), approx=True)
            gain_down[at] = gain
            above[at] = tau_of(at) - gain * chip_c[at, 0]
        face_gain[0] = zero
        face_gain[chips] = zero
        for at in range(1, chips):
            face_gain[at] = pl.reciprocal(1.0 + below[at] + above[at], approx=True)

    def fix_body(z, carry):
        first, last = slice(0, 1), slice(slab - 1, slab)
        to_lower = (SECTION_RATE / RZ) * root[z, first] * halo[STEPS, 0, z]
        to_upper = (SECTION_RATE / RZ) * root[z, last] * halo[STEPS, 1, z]
        w_lower[z, first] = to_lower
        w_upper[z, last] = to_upper
        centre[z, first] = centre[z, first] - to_lower
        centre[z, last] = centre[z, last] - to_upper
        return carry

    keep_table = [1.0 - upt_tab[index] for index in range(upt_tab.shape[0])]

    def cell_body(z, carry):
        there = mask[z] != 0
        keep[z] = jnp.where(there, lookup(layer[z], keep_table), 1.0)
        source[z] = jnp.where(there, source[z], 0.0)
        return carry

    def forward(step, ranges):
        def body(z, carries):
            done = []
            for (lo, hi), (moved, first) in zip(ranges, carries):
                span = slice(lo, hi)
                size = hi - lo
                row = lax.broadcasted_iota(jnp.int32, (size, cols), 0)
                now = state[z, span]
                before = halo[step, 0, z] if lo == 0 else state[z, lo - 1:lo]
                behind = halo[step, 1, z] if hi == slab else state[z, hi:hi + 1]
                lower = jnp.where(row == 0, before, pltpu.roll(now, 1, 0))
                upper = jnp.where(row == size - 1, behind, pltpu.roll(now, size - 1, 0))
                across = w_left[z, span] * pltpu.roll(now, 1, 1) + w_right[z, span] * pltpu.roll(now, cols - 1, 1)
                along = w_lower[z, span] * lower + w_upper[z, span] * upper
                explicit = (centre[z, span] * now + along) + across
                value = explicit + moved
                part[z, span] = recip[z, span] * value
                done.append((ratio[z, span] * value, first + prodr[z, span] * value))
            return tuple(done)

        zeros = [jnp.zeros((hi - lo, cols), f32) for lo, hi in ranges]
        sums = lax.fori_loop(0, m, body, tuple((zero, zero) for zero in zeros), unroll=16)
        for (lo, hi), (_, first) in zip(ranges, sums):
            span = slice(lo, hi)
            dev_v[step, 0, span] = first
            dev_v[step, 1, span] = part[m - 1, span]

    def forward_mate_first(step, group):
        lower, upper = ((q, half), (half, half + q)) if group == 0 else ((0, q), (half + q, slab))

        def run(first, second):
            forward(step, (first,))
            pair_v_copy(step, group).start()
            forward(step, (second,))

        pl.when(low)(lambda: run(upper, lower))
        pl.when(jnp.logical_not(low))(lambda: run(lower, upper))

    def combine(step, group):
        at = kept(group)
        pair_v_copy(step, group).wait_recv()
        mine = [dev_v[step, row, lines(True, group)] for row in range(2)]
        his = [pair_v[step, row, at] for row in range(2)]
        first_l, last_l = [jnp.where(low, a, b) for a, b in zip(mine, his)]
        first_u, last_u = [jnp.where(low, b, a) for a, b in zip(mine, his)]
        gap = last_l - first_u
        first = links[3, at] * (first_l - links[1, at] * gap)
        last = links[4, at] * (last_u + links[2, at] * gap)
        found[0, at], found[1, at], found[2, at] = links[0, at] * gap, first, last

        if step == 0:
            raw_v[chip, group, 0] = jnp.where(last_chip, last, first)
            raw_v[chip, group, 1] = jnp.where(last_chip, first, last)
            to_peers(2, lambda count, to: raw_copy(count, group, chip, to).start())

        if step > 0:
            fold_out[step, group, 0] = first - gain_down[chip, at] * last
            fold_out[step, group, 1] = last - gain_up[chip, at] * first
            for to in peers:
                fold_copy(step, group, chip, to).start()

    def interfaces(step, group):
        at = kept(group)

        if step == 0:
            from_peers(2, lambda count, sender: raw_copy(count, group, sender, sender).wait_recv())
            below = jnp.zeros((q, cols), f32)
            above = jnp.zeros((q, cols), f32)
            for sender in range(chips - 1):
                there = raw_v[sender, group, 1]
                if sender > 0:
                    there = there + gain_up[sender, at] * (below - raw_v[sender, group, 0])
                below = jnp.where(sender < chip, there, below)
            for sender in range(chips - 1, 0, -1):
                if sender == chips - 1:
                    there = raw_v[sender, group, 1]
                else:
                    there = raw_v[sender, group, 0] - gain_down[sender, at] * (raw_v[sender, group, 1] - above)
                above = jnp.where(sender > chip, there, above)
            heard[0], heard[1] = below, above

        if step > 0:
            for sender in peers:
                fold_copy(step, group, sender, sender).wait_recv()
            below = jnp.zeros((q, cols), f32)
            above = jnp.zeros((q, cols), f32)
            for sender in range(chips - 1):
                there = fold_v[step, sender, group] + gain_up[sender, at] * below
                below = jnp.where(sender < chip, there, below)
            for sender in range(chips - 1, 0, -1):
                there = fold_v[step, sender, group] + gain_down[sender, at] * above
                above = jnp.where(sender > chip, there, above)
            heard[0], heard[1] = below, above

        below, above = heard[0], heard[1]
        gap, first, last = found[0, at], found[1, at], found[2, at]
        from_low = last + gain_up[chip, at] * (below - first)
        from_high = first - gain_down[chip, at] * (last - above)
        flow_low = (below - from_high) * face_gain[chip, at] * links[3, at]
        flow_high = (from_low - above) * face_gain[chip + 1, at] * links[4, at]
        flow_mid = gap + links[1, at] * flow_low + links[2, at] * flow_high
        flow[step, 0, lines(True, group)] = flow_mid
        flow[step, 1, lines(True, group)] = jnp.where(low, flow_low, flow_high)
        back_out[step, group, 0] = flow_mid
        back_out[step, group, 1] = jnp.where(low, flow_high, flow_low)
        back_copy(step, group, True).start()

    def backward(step, ranges):
        lows = []
        highs = []
        for lo, hi in ranges:
            span = slice(lo, hi)
            mid, outer = flow[step, 0, span], flow[step, 1, span]
            lows.append(jnp.where(low, outer, mid))
            highs.append(-jnp.where(low, mid, outer))

        def body(at, carries):
            z = m - 1 - at
            done = []
            for (lo, hi), entering, later in zip(ranges, lows, carries):
                span = slice(lo, hi)
                solved = part[z, span] + prodr[z, span] * entering + ratio[z, span] * later
                after = keep[z, span] * solved + source[z, span]
                state[z, span] = after
                if lo == 0:
                    edge[step, 0, z] = after[0:1]
                if hi == slab:
                    edge[step, 1, z] = after[hi - lo - 1:hi - lo]
                done.append(solved)
            return tuple(done)

        lax.fori_loop(0, m, body, tuple(highs), unroll=8)

    combine_coefficients()
    xs_wait(STEPS)
    lax.fori_loop(0, m, fix_body, 0, unroll=8)
    conc_load.wait()

    def backward_part(step, group, mine):
        lower, upper = ((q, half), (half, half + q)) if group == 0 else ((0, q), (half + q, slab))
        pl.when(low == mine)(lambda: backward(step, (lower,)))
        pl.when(low != mine)(lambda: backward(step, (upper,)))

    for step in range(STEPS):
        order = (1, 0) if step == 0 else (0, 1)
        for group in order:
            if group == 1:
                xs_wait(step)
            if step == STEPS - 1 and group == 1:
                forward_mate_first(step, group)
            else:
                forward(step, spans[group])
                pair_v_copy(step, group).start()
            if step > 0:
                combine(step, group)
        if step == 0:
            for group in order:
                combine(step, group)
            prod_load.wait()
            lax.fori_loop(0, m, cell_body, 0, unroll=8)
            gather_coefficients()
        if step < STEPS - 1:
            for group in order:
                interfaces(step, group)
                backward_part(step, group, True)
                back_copy(step, group, False).wait_recv()
                backward_part(step, group, False)
                if group == 1:
                    xs_start(step + 1, [edge.at[step, at, :, 0] for at in range(2)])
        else:
            for group in order:
                interfaces(step, group)
            for group in order:
                back_copy(step, group, False).wait_recv()
                backward(step, spans[group])

    for at in range(2):
        @pl.when(sides[at][0])
        def _(at=at):
            for slot in range(STEPS + 1):
                xs_copy(slot, at).wait_send()

        @pl.when(has_outer)
        def _(at=at):
            ax_copy(at).wait_send()

    face_copy().wait_send()

    to_peers(3, lambda count, to: coef_copy(count, chip, to).wait_send())

    def finish(group):
        pair_c_copy(group).wait_send()
        to_peers(2, lambda count, to: raw_copy(count, group, chip, to).wait_send())
        for step in range(STEPS):
            pair_v_copy(step, group).wait_send()
            back_copy(step, group, True).wait_send()
            if step > 0:
                for to in peers:
                    fold_copy(step, group, chip, to).wait_send()

    loop_groups(finish)


def on_device(n_ax, n_xs, conc, mask, layer, stiff, prod, diff_tab, upt_tab):
    m, slab, cols = conc.shape
    chips = n_ax // 2
    half, q = slab // 2, slab // 4
    f32 = jnp.float32
    cells = pltpu.VMEM((m, slab, cols), f32)
    labels = pltpu.VMEM((m, slab, cols), jnp.int32)
    dma = pltpu.SemaphoreType.DMA
    vmem = lambda *shape: pltpu.VMEM(shape, f32)
    hbm_spec = pl.BlockSpec(memory_space=pltpu.HBM)
    return pl.pallas_call(
        functools.partial(kernel, n_ax, n_xs),
        out_shape=pltpu.VMEM((m, slab, cols), f32),
        in_specs=[hbm_spec] * 7,
        out_specs=pl.BlockSpec(memory_space=pltpu.VMEM),
        scratch_shapes=[
            pltpu.SMEM(diff_tab.shape, f32), pltpu.SMEM(upt_tab.shape, f32),
            pltpu.VMEM((2, slab, cols), jnp.int32), pltpu.VMEM((2, slab, cols), jnp.int32),
            vmem(2, slab, cols), vmem(2, slab, cols),
            pltpu.VMEM((2, m, cols), jnp.int32), pltpu.VMEM((2, m, cols), jnp.int32),
            vmem(2, m, cols), vmem(2, m, cols),
            labels, labels, cells, cells, vmem(m + 1, slab, cols),
            cells, cells, cells, cells, cells, cells, cells, cells, cells, cells,
            vmem(STEPS, 2, m, 1, cols), vmem(STEPS + 1, 2, m, 1, cols),
            vmem(2, half, cols), vmem(2, half, cols),
            vmem(3, slab, cols), vmem(3, half, cols), vmem(chips, 3, half, cols),
            vmem(5, half, cols), vmem(chips, half, cols), vmem(chips, half, cols), vmem(chips + 1, half, cols),
            vmem(STEPS, 2, slab, cols), vmem(STEPS, 2, half, cols),
            vmem(chips, 2, 2, q, cols), vmem(STEPS, chips, 2, q, cols), vmem(STEPS, 2, 2, q, cols),
            vmem(3, half, cols), vmem(2, q, cols),
            vmem(STEPS, 2, slab, cols), vmem(STEPS, 2, 2, q, cols),
            dma((16 + 3 * LOADS,)), dma((STEPS + 1, 2)), dma((STEPS + 1, 2)), dma((2,)), dma((2,)), dma((2,)),
            dma((2,)), dma((2,)), dma((STEPS, 2)), dma((STEPS, 2)), dma((STEPS, 2)), dma((STEPS, 2)),
            dma((chips,)), dma((chips,)), dma((STEPS, 2, chips)), dma((STEPS, 2, chips)),
        ],
        compiler_params=pltpu.CompilerParams(
            collective_id=0, has_side_effects=True, vmem_limit_bytes=56 * 1024 * 1024
        ),
    )(conc, mask, layer, stiff, prod, diff_tab, upt_tab)


def solution(mesh):
    cells = P("ax", "xs", None)
    return jax.shard_map(
        functools.partial(on_device, mesh.shape["ax"], mesh.shape["xs"]),
        mesh=mesh, in_specs=(cells,) * 5 + (P(), P()), out_specs=cells, check_vma=False,
    )
```

```python
import functools

import jax
import jax.numpy as jnp
from jax import lax
from jax.experimental import pallas as pl
from jax.experimental.pallas import tpu as pltpu
from jax.sharding import PartitionSpec as P

STEPS = 2
RZ = 3072
SECTION_RATE = 0.05
LOADS = 4
AHEAD = 4
GREET = 1
CONC_AT = 1
PROD_AT = 2
MESH = pl.DeviceIdType.MESH


def lookup(labels, table):
    found = jnp.full(labels.shape, table[0], jnp.float32)
    for index in range(1, len(table)):
        found = jnp.where(labels == index, table[index], found)
    return found


def kernel(
    n_ax, n_xs,
    conc_hbm, mask_hbm, layer_hbm, stiff_hbm, prod_hbm, diff_hbm, upt_hbm,
    state,
    diff_tab, upt_tab,
    mask_face, layer_face, stiff_face, face, mask_rim, layer_rim, stiff_rim, rim, mask, layer, stiff, source, root, ratio, recip, prodr, part, w_lower, w_upper, w_left, w_right, centre, keep,
    edge, halo, beyond, mate_face, dev_c, pair_c, chip_c, links, gain_up, gain_down, face_gain,
    dev_v, pair_v, raw_v, fold_v, fold_out, found, heard, flow, back_out,
    in_sem, xs_send, xs_recv, ax_send, ax_recv, face_sem,
    pc_send, pc_recv, pv_send, pv_recv, bk_send, bk_recv, cc_send, cc_recv, cv_send, cv_recv,
):
    m, slab, cols = conc_hbm.shape
    chips = n_ax // 2
    half = slab // 2
    q = slab // 4
    f32 = jnp.float32
    me = lax.axis_index("ax")
    mx = lax.axis_index("xs")
    chip = lax.div(me, 2)
    core = lax.rem(me, 2)
    low = core == 0
    mate = {"ax": me + 1 - 2 * core}

    inside, ends = ((q, half + q),), ((0, q), (half + q, slab))

    def lines(mine, group):
        inner = jnp.where(low, q, half) if mine else jnp.where(low, half, q)
        outer = jnp.where(low, 0, half + q) if mine else jnp.where(low, half + q, 0)
        return pl.ds(pl.multiple_of(jnp.where(group == 0, inner, outer), 8), q)

    spans = (inside, ends)

    def halfway(group):
        return pl.ds(pl.multiple_of(jnp.where(low == (group == 0), q, 0), 8), q)

    def kept(group):
        return pl.ds(pl.multiple_of(group * q, 8), q)

    def local(src, dst, at):
        return pltpu.make_async_copy(src, dst, in_sem.at[at])

    chunk = m // LOADS
    arrays = [
        (mask_hbm, mask, mask_face, mask_rim), (layer_hbm, layer, layer_face, layer_rim),
        (stiff_hbm, stiff, stiff_face, stiff_rim),
    ]
    tables = [local(diff_hbm, diff_tab, 0), local(upt_hbm, upt_tab, 1)]
    face_loads = [
        local(src.at[z], dst.at[k], 2 + 2 * at + k)
        for at, (src, _, dst, _) in enumerate(arrays) for k, z in enumerate((0, m - 1))
    ]
    rim_loads = [
        local(src.at[:, line], dst.at[k], 8 + 2 * at + k)
        for at, (src, _, _, dst) in enumerate(arrays) for k, line in enumerate((0, slab - 1))
    ]
    conc_load = local(conc_hbm, state, 14)
    prod_load = local(prod_hbm, source, 15)

    def part_loads(at):
        planes = pl.ds(at * chunk, chunk)
        return [
            local(src.at[planes], dst.at[planes], 16 + 3 * at + k) for k, (src, dst, _, _) in enumerate(arrays)
        ]

    sides = (
        (mx > 0, {"xs": mx - 1}),
        (mx < n_xs - 1, {"xs": mx + 1}),
        (me > 0, {"ax": me - 1}),
        (me < n_ax - 1, {"ax": me + 1}),
    )
    last_chip = chip == chips - 1
    between = (chip > 0) & (chip < chips - 1)
    peers = [lax.rem(chip + reach, chips) for reach in range(chips - 1, 0, -1)]
    greeted = list(sides) + [(True, {"ax": 2 * to + core}) for to in peers]
    barrier = pltpu.get_barrier_semaphore()
    for there, peer in greeted:
        @pl.when(there)
        def _(peer=peer):
            pl.semaphore_signal(barrier, inc=1, device_id=peer, device_id_type=MESH)

    for load in tables + part_loads(0) + face_loads + rim_loads:
        load.start()
    for at in range(1, AHEAD):
        for load in part_loads(at):
            load.start()

    for at in range(2):
        @pl.when(jnp.logical_not(sides[at][0]))
        def _(at=at):
            for slot in range(STEPS + 1):
                halo[slot, at] = jnp.zeros((m, 1, cols), f32)

        @pl.when((chip == 0) if at == 0 else (chip == chips - 1))
        def _(at=at):
            beyond[at] = jnp.zeros((half, cols), f32)

    root[m] = jnp.zeros((slab, cols), f32)

    def xs_copy(slot, at, src=None):
        return pltpu.make_async_remote_copy(
            src_ref=rim.at[at] if src is None else src, dst_ref=halo.at[slot, 1 - at, :, 0],
            send_sem=xs_send.at[slot, at], recv_sem=xs_recv.at[slot, 1 - at],
            device_id=sides[at][1], device_id_type=MESH,
        )

    def xs_start(slot, sources):
        for at in range(2):
            @pl.when(sides[at][0])
            def _(at=at):
                xs_copy(slot, at, sources[at]).start()

    def xs_wait(slot):
        for at in range(2):
            @pl.when(sides[at][0])
            def _(at=at):
                xs_copy(slot, 1 - at).wait_recv()

    def ax_copy(to):
        step_to = jnp.where(low, -1, 1)
        return pltpu.make_async_remote_copy(
            src_ref=face.at[core, pl.ds(to * half, half)], dst_ref=beyond.at[1 - core],
            send_sem=ax_send.at[to], recv_sem=ax_recv.at[1 - core],
            device_id={"ax": 2 * (chip + step_to) + to}, device_id_type=MESH,
        )

    def ax_landed(at):
        return pltpu.make_async_remote_copy(
            src_ref=face.at[0, pl.ds(0, half)], dst_ref=beyond.at[at],
            send_sem=ax_send.at[0], recv_sem=ax_recv.at[at], device_id=mate, device_id_type=MESH,
        )

    def face_copy():
        return pltpu.make_async_remote_copy(
            src_ref=face.at[:, pl.ds(pl.multiple_of((1 - core) * half, 8), half)], dst_ref=mate_face,
            send_sem=face_sem.at[0], recv_sem=face_sem.at[1], device_id=mate, device_id_type=MESH,
        )

    has_outer = jnp.where(low, chip > 0, chip < chips - 1)

    for load in tables:
        load.wait()
    scaled_table = [RZ * diff_tab[index] for index in range(diff_tab.shape[0])]

    def scaled_root(mask_now, layer_now, stiff_now):
        square = lookup(layer_now, scaled_table) * stiff_now
        return jnp.where(mask_now != 0, square * lax.rsqrt(square), 0.0)

    row_at = lax.broadcasted_iota(jnp.int32, (slab, cols), 0)
    col_at = lax.broadcasted_iota(jnp.int32, (slab, cols), 1)

    def root_part(at, carry):
        @pl.when(at == GREET)
        def _():
            for load in face_loads + rim_loads:
                load.wait()
            for end in range(2):
                face[end] = scaled_root(mask_face[end], layer_face[end], stiff_face[end])
                rim[end] = scaled_root(mask_rim[end], layer_rim[end], stiff_rim[end])
            pl.semaphore_wait(barrier, sum(jnp.where(there, 1, 0) for there, _ in greeted))
            @pl.when(has_outer)
            def _():
                for to in range(2):
                    ax_copy(to).start()

            face_copy().start()
            xs_start(STEPS, [rim.at[0], rim.at[1]])
            xs_start(0, [conc_hbm.at[:, 0], conc_hbm.at[:, slab - 1]])

        for load in part_loads(at):
            load.wait()

        if AHEAD < LOADS:
            @pl.when(at + AHEAD < LOADS)
            def _():
                for load in part_loads(at + AHEAD):
                    load.start()

        @pl.when(at == CONC_AT)
        def _():
            conc_load.start()

        @pl.when(at == PROD_AT)
        def _():
            prod_load.start()

        for offset in range(chunk):
            z = at * chunk + offset
            value = scaled_root(mask[z], layer[z], stiff[z])
            root[z] = value
        return carry

    lax.fori_loop(0, LOADS, root_part, 0)

    def factor_body(z, carry):
        excess, product, total = carry
        band = root[z] * root[z + 1]
        inverse = pl.reciprocal(excess + band, approx=True)
        ratio_now = band * inverse
        scaled = product * inverse
        ratio[z] = ratio_now
        recip[z] = inverse
        prodr[z] = scaled
        return 1.0 + ratio_now * excess, product * ratio_now, total + product * scaled

    ones = jnp.ones((slab, cols), f32)
    _, _, total = lax.fori_loop(0, m, factor_body, (ones, ones, 0.0 * ones), unroll=8)
    sigma = recip[m - 1]
    ratio[m - 1] = sigma

    dev_c[0] = total
    dev_c[1] = prodr[m - 1]
    dev_c[2] = sigma

    def weight_body(z, carry):
        value = root[z]
        scaled = (SECTION_RATE / RZ) * value
        to_lower = jnp.where(row_at == 0, 0.0, scaled * pltpu.roll(value, 1, 0))
        to_left = jnp.where(col_at == 0, 0.0, scaled * pltpu.roll(value, 1, 1))
        to_upper = pltpu.roll(to_lower, slab - 1, 0)
        to_right = pltpu.roll(to_left, cols - 1, 1)
        w_lower[z], w_upper[z], w_left[z], w_right[z] = to_lower, to_upper, to_left, to_right
        centre[z] = 1.0 - ((to_lower + to_upper) + (to_left + to_right))
        return carry

    def mate_copy(src, dst, send, recv):
        return pltpu.make_async_remote_copy(
            src_ref=src, dst_ref=dst, send_sem=send, recv_sem=recv, device_id=mate, device_id_type=MESH
        )

    def pair_c_copy(group):
        return mate_copy(
            dev_c.at[:, lines(False, group)], pair_c.at[:, kept(group)], pc_send.at[group], pc_recv.at[group]
        )

    def pair_v_copy(step, group):
        return mate_copy(
            dev_v.at[step, :, lines(False, group)], pair_v.at[step, :, kept(group)],
            pv_send.at[step, group], pv_recv.at[step, group],
        )

    def back_copy(step, group, mine):
        return mate_copy(
            back_out.at[step, group], flow.at[step, :, lines(mine, group)],
            bk_send.at[step, group], bk_recv.at[step, group],
        )

    def far_copy(src, dst, send, recv, to):
        return pltpu.make_async_remote_copy(
            src_ref=src, dst_ref=dst, send_sem=send, recv_sem=recv,
            device_id={"ax": 2 * to + core}, device_id_type=MESH,
        )

    def coef_copy(count, sender, to):
        rows = pl.ds(3 - count, count)
        return far_copy(
            chip_c.at[chip, rows], chip_c.at[sender, rows], cc_send.at[to], cc_recv.at[sender], to
        )

    def raw_copy(count, group, sender, to):
        rows = pl.ds(2 - count, count)
        return far_copy(
            raw_v.at[chip, group, rows], raw_v.at[sender, group, rows],
            cv_send.at[0, group, to], cv_recv.at[0, group, sender], to,
        )

    def fold_copy(step, group, sender, to):
        return far_copy(
            fold_out.at[step, group, jnp.where(to > chip, 1, 0)], fold_v.at[step, sender, group],
            cv_send.at[step, group, to], cv_recv.at[step, group, sender], to,
        )

    def to_peers(count, act):
        @pl.when(between)
        def _():
            for to in peers:
                act(count, to)

        @pl.when(jnp.logical_not(between))
        def _():
            for to in peers:
                act(1, to)

    def from_peers(count, act):
        for sender in range(chips):
            @pl.when(chip != sender)
            def _(sender=sender):
                act(count if 0 < sender < chips - 1 else 1, sender)

    def tau_of(at):
        return chip_c[at, 2 if at == chips - 1 else 1]

    def sigma_of(at):
        return chip_c[at, 1 if at == chips - 1 else 2]

    def loop_groups(act):
        def body(group, carry):
            act(group)
            return carry

        lax.fori_loop(0, 2, body, 0)

    loop_groups(lambda group: pair_c_copy(group).start())
    lax.fori_loop(0, m, weight_body, 0, unroll=8)

    def combine_coefficients():
        def one(group):
            pair_c_copy(group).wait_recv()
            at = kept(group)
            mine = [dev_c[row, lines(True, group)] for row in range(3)]
            his = [pair_c[row, at] for row in range(3)]
            tau_l, rho_l, sigma_l = [jnp.where(low, a, b) for a, b in zip(mine, his)]
            tau_u, rho_u, sigma_u = [jnp.where(low, b, a) for a, b in zip(mine, his)]
            near = halfway(group)
            face_l, face_u = [
                [jnp.where(low == lower, face[k, lines(True, group)], mate_face[k, near]) for k in range(2)]
                for lower in (True, False)
            ]
            band = face_l[1] * face_u[0]
            joint = band * pl.reciprocal(1.0 + band * (sigma_l + tau_u), approx=True)
            link_l, link_u = rho_l * joint, rho_u * joint
            band_low, band_high = beyond[0, near] * face_l[0], face_u[1] * beyond[1, near]
            scale_low, scale_high = jnp.sqrt(band_low), jnp.sqrt(band_high)
            links[0, at], links[1, at], links[2, at] = joint, link_l, link_u
            links[3, at], links[4, at] = scale_low, scale_high
            tau, sigma = band_low * (tau_l - rho_l * link_l), band_high * (sigma_u - rho_u * link_u)
            chip_c[chip, 0, at] = (scale_low * scale_high) * (rho_l * link_u)
            chip_c[chip, 1, at] = jnp.where(last_chip, sigma, tau)
            chip_c[chip, 2, at] = jnp.where(last_chip, tau, sigma)

        for at in range(2):
            @pl.when((chip > 0) if at == 0 else (chip < chips - 1))
            def _(at=at):
                ax_landed(at).wait_recv()

        face_copy().wait_recv()
        loop_groups(one)
        to_peers(3, lambda count, to: coef_copy(count, chip, to).start())

    def gather_coefficients():
        from_peers(3, lambda count, sender: coef_copy(count, sender, sender).wait_recv())
        zero = jnp.zeros((half, cols), f32)
        below, above = [zero] * (chips + 1), [zero] * (chips + 1)
        gain_up[0] = zero
        gain_up[chips - 1] = zero
        gain_down[0] = zero
        gain_down[chips - 1] = zero
        below[1] = sigma_of(0)
        for at in range(1, chips - 1):
            gain = chip_c[at, 0] * pl.reciprocal(1.0 + below[at] + tau_of(at), approx=True)
            gain_up[at] = gain
            below[at + 1] = sigma_of(at) - gain * chip_c[at, 0]
        above[chips - 1] = tau_of(chips - 1)
        for at in range(chips - 2, 0, -1):
            gain = chip_c[at, 0] * pl.reciprocal(1.0 + above[at + 1] + sigma_of(at), approx=True)
            gain_down[at] = gain
            above[at] = tau_of(at) - gain * chip_c[at, 0]
        face_gain[0] = zero
        face_gain[chips] = zero
        for at in range(1, chips):
            face_gain[at] = pl.reciprocal(1.0 + below[at] + above[at], approx=True)

    def fix_body(z, carry):
        first, last = slice(0, 1), slice(slab - 1, slab)
        to_lower = (SECTION_RATE / RZ) * root[z, first] * halo[STEPS, 0, z]
        to_upper = (SECTION_RATE / RZ) * root[z, last] * halo[STEPS, 1, z]
        w_lower[z, first] = to_lower
        w_upper[z, last] = to_upper
        centre[z, first] = centre[z, first] - to_lower
        centre[z, last] = centre[z, last] - to_upper
        return carry

    keep_table = [1.0 - upt_tab[index] for index in range(upt_tab.shape[0])]

    def cell_body(z, carry):
        there = mask[z] != 0
        keep[z] = jnp.where(there, lookup(layer[z], keep_table), 1.0)
        source[z] = jnp.where(there, source[z], 0.0)
        return carry

    def forward(step, ranges):
        def body(z, carries):
            done = []
            for (lo, hi), (moved, first) in zip(ranges, carries):
                span = slice(lo, hi)
                size = hi - lo
                row = lax.broadcasted_iota(jnp.int32, (size, cols), 0)
                now = state[z, span]
                before = halo[step, 0, z] if lo == 0 else state[z, lo - 1:lo]
                behind = halo[step, 1, z] if hi == slab else state[z, hi:hi + 1]
                lower = jnp.where(row == 0, before, pltpu.roll(now, 1, 0))
                upper = jnp.where(row == size - 1, behind, pltpu.roll(now, size - 1, 0))
                across = w_left[z, span] * pltpu.roll(now, 1, 1) + w_right[z, span] * pltpu.roll(now, cols - 1, 1)
                along = w_lower[z, span] * lower + w_upper[z, span] * upper
                explicit = (centre[z, span] * now + along) + across
                value = explicit + moved
                part[z, span] = recip[z, span] * value
                done.append((ratio[z, span] * value, first + prodr[z, span] * value))
            return tuple(done)

        zeros = [jnp.zeros((hi - lo, cols), f32) for lo, hi in ranges]
        sums = lax.fori_loop(0, m, body, tuple((zero, zero) for zero in zeros), unroll=16)
        for (lo, hi), (_, first) in zip(ranges, sums):
            span = slice(lo, hi)
            dev_v[step, 0, span] = first
            dev_v[step, 1, span] = part[m - 1, span]

    def forward_mate_first(step, group):
        lower, upper = ((q, half), (half, half + q)) if group == 0 else ((0, q), (half + q, slab))

        def run(first, second):
            forward(step, (first,))
            pair_v_copy(step, group).start()
            forward(step, (second,))

        pl.when(low)(lambda: run(upper, lower))
        pl.when(jnp.logical_not(low))(lambda: run(lower, upper))

    def combine(step, group):
        at = kept(group)
        pair_v_copy(step, group).wait_recv()
        mine = [dev_v[step, row, lines(True, group)] for row in range(2)]
        his = [pair_v[step, row, at] for row in range(2)]
        first_l, last_l = [jnp.where(low, a, b) for a, b in zip(mine, his)]
        first_u, last_u = [jnp.where(low, b, a) for a, b in zip(mine, his)]
        gap = last_l - first_u
        first = links[3, at] * (first_l - links[1, at] * gap)
        last = links[4, at] * (last_u + links[2, at] * gap)
        found[0, at], found[1, at], found[2, at] = links[0, at] * gap, first, last

        if step == 0:
            raw_v[chip, group, 0] = jnp.where(last_chip, last, first)
            raw_v[chip, group, 1] = jnp.where(last_chip, first, last)
            to_peers(2, lambda count, to: raw_copy(count, group, chip, to).start())

        if step > 0:
            fold_out[step, group, 0] = first - gain_down[chip, at] * last
            fold_out[step, group, 1] = last - gain_up[chip, at] * first
            for to in peers:
                fold_copy(step, group, chip, to).start()

    def interfaces(step, group):
        at = kept(group)

        if step == 0:
            from_peers(2, lambda count, sender: raw_copy(count, group, sender, sender).wait_recv())
            below = jnp.zeros((q, cols), f32)
            above = jnp.zeros((q, cols), f32)
            for sender in range(chips - 1):
                there = raw_v[sender, group, 1]
                if sender > 0:
                    there = there + gain_up[sender, at] * (below - raw_v[sender, group, 0])
                below = jnp.where(sender < chip, there, below)
            for sender in range(chips - 1, 0, -1):
                if sender == chips - 1:
                    there = raw_v[sender, group, 1]
                else:
                    there = raw_v[sender, group, 0] - gain_down[sender, at] * (raw_v[sender, group, 1] - above)
                above = jnp.where(sender > chip, there, above)
            heard[0], heard[1] = below, above

        if step > 0:
            for sender in peers:
                fold_copy(step, group, sender, sender).wait_recv()
            below = jnp.zeros((q, cols), f32)
            above = jnp.zeros((q, cols), f32)
            for sender in range(chips - 1):
                there = fold_v[step, sender, group] + gain_up[sender, at] * below
                below = jnp.where(sender < chip, there, below)
            for sender in range(chips - 1, 0, -1):
                there = fold_v[step, sender, group] + gain_down[sender, at] * above
                above = jnp.where(sender > chip, there, above)
            heard[0], heard[1] = below, above

        below, above = heard[0], heard[1]
        gap, first, last = found[0, at], found[1, at], found[2, at]
        from_low = last + gain_up[chip, at] * (below - first)
        from_high = first - gain_down[chip, at] * (last - above)
        flow_low = (below - from_high) * face_gain[chip, at] * links[3, at]
        flow_high = (from_low - above) * face_gain[chip + 1, at] * links[4, at]
        flow_mid = gap + links[1, at] * flow_low + links[2, at] * flow_high
        flow[step, 0, lines(True, group)] = flow_mid
        flow[step, 1, lines(True, group)] = jnp.where(low, flow_low, flow_high)
        back_out[step, group, 0] = flow_mid
        back_out[step, group, 1] = jnp.where(low, flow_high, flow_low)
        back_copy(step, group, True).start()

    def backward(step, ranges):
        lows = []
        highs = []
        for lo, hi in ranges:
            span = slice(lo, hi)
            mid, outer = flow[step, 0, span], flow[step, 1, span]
            lows.append(jnp.where(low, outer, mid))
            highs.append(-jnp.where(low, mid, outer))

        def body(at, carries):
            z = m - 1 - at
            done = []
            for (lo, hi), entering, later in zip(ranges, lows, carries):
                span = slice(lo, hi)
                solved = part[z, span] + prodr[z, span] * entering + ratio[z, span] * later
                after = keep[z, span] * solved + source[z, span]
                state[z, span] = after
                if lo == 0:
                    edge[step, 0, z] = after[0:1]
                if hi == slab:
                    edge[step, 1, z] = after[hi - lo - 1:hi - lo]
                done.append(solved)
            return tuple(done)

        lax.fori_loop(0, m, body, tuple(highs), unroll=8)

    combine_coefficients()
    xs_wait(STEPS)
    lax.fori_loop(0, m, fix_body, 0, unroll=8)
    conc_load.wait()

    def backward_part(step, group, mine):
        lower, upper = ((q, half), (half, half + q)) if group == 0 else ((0, q), (half + q, slab))
        pl.when(low == mine)(lambda: backward(step, (lower,)))
        pl.when(low != mine)(lambda: backward(step, (upper,)))

    for step in range(STEPS):
        order = (1, 0) if step == 0 else (0, 1)
        for group in order:
            if group == 1:
                xs_wait(step)
            if step == STEPS - 1 and group == 1:
                forward_mate_first(step, group)
            else:
                forward(step, spans[group])
                pair_v_copy(step, group).start()
            if step > 0:
                combine(step, group)
        if step == 0:
            for group in order:
                combine(step, group)
            prod_load.wait()
            lax.fori_loop(0, m, cell_body, 0, unroll=8)
            gather_coefficients()
        if step < STEPS - 1:
            for group in order:
                interfaces(step, group)
                backward_part(step, group, True)
                back_copy(step, group, False).wait_recv()
                backward_part(step, group, False)
                if group == 1:
                    xs_start(step + 1, [edge.at[step, at, :, 0] for at in range(2)])
        else:
            for group in order:
                interfaces(step, group)
                backward_part(step, group, True)
            for group in order:
                back_copy(step, group, False).wait_recv()
                backward_part(step, group, False)

    for at in range(2):
        @pl.when(sides[at][0])
        def _(at=at):
            for slot in range(STEPS + 1):
                xs_copy(slot, at).wait_send()

        @pl.when(has_outer)
        def _(at=at):
            ax_copy(at).wait_send()

    face_copy().wait_send()

    to_peers(3, lambda count, to: coef_copy(count, chip, to).wait_send())

    def finish(group):
        pair_c_copy(group).wait_send()
        to_peers(2, lambda count, to: raw_copy(count, group, chip, to).wait_send())
        for step in range(STEPS):
            pair_v_copy(step, group).wait_send()
            back_copy(step, group, True).wait_send()
            if step > 0:
                for to in peers:
                    fold_copy(step, group, chip, to).wait_send()

    loop_groups(finish)


def on_device(n_ax, n_xs, conc, mask, layer, stiff, prod, diff_tab, upt_tab):
    m, slab, cols = conc.shape
    chips = n_ax // 2
    half, q = slab // 2, slab // 4
    f32 = jnp.float32
    cells = pltpu.VMEM((m, slab, cols), f32)
    labels = pltpu.VMEM((m, slab, cols), jnp.int32)
    dma = pltpu.SemaphoreType.DMA
    vmem = lambda *shape: pltpu.VMEM(shape, f32)
    hbm_spec = pl.BlockSpec(memory_space=pltpu.HBM)
    return pl.pallas_call(
        functools.partial(kernel, n_ax, n_xs),
        out_shape=pltpu.VMEM((m, slab, cols), f32),
        in_specs=[hbm_spec] * 7,
        out_specs=pl.BlockSpec(memory_space=pltpu.VMEM),
        scratch_shapes=[
            pltpu.SMEM(diff_tab.shape, f32), pltpu.SMEM(upt_tab.shape, f32),
            pltpu.VMEM((2, slab, cols), jnp.int32), pltpu.VMEM((2, slab, cols), jnp.int32),
            vmem(2, slab, cols), vmem(2, slab, cols),
            pltpu.VMEM((2, m, cols), jnp.int32), pltpu.VMEM((2, m, cols), jnp.int32),
            vmem(2, m, cols), vmem(2, m, cols),
            labels, labels, cells, cells, vmem(m + 1, slab, cols),
            cells, cells, cells, cells, cells, cells, cells, cells, cells, cells,
            vmem(STEPS, 2, m, 1, cols), vmem(STEPS + 1, 2, m, 1, cols),
            vmem(2, half, cols), vmem(2, half, cols),
            vmem(3, slab, cols), vmem(3, half, cols), vmem(chips, 3, half, cols),
            vmem(5, half, cols), vmem(chips, half, cols), vmem(chips, half, cols), vmem(chips + 1, half, cols),
            vmem(STEPS, 2, slab, cols), vmem(STEPS, 2, half, cols),
            vmem(chips, 2, 2, q, cols), vmem(STEPS, chips, 2, q, cols), vmem(STEPS, 2, 2, q, cols),
            vmem(3, half, cols), vmem(2, q, cols),
            vmem(STEPS, 2, slab, cols), vmem(STEPS, 2, 2, q, cols),
            dma((16 + 3 * LOADS,)), dma((STEPS + 1, 2)), dma((STEPS + 1, 2)), dma((2,)), dma((2,)), dma((2,)),
            dma((2,)), dma((2,)), dma((STEPS, 2)), dma((STEPS, 2)), dma((STEPS, 2)), dma((STEPS, 2)),
            dma((chips,)), dma((chips,)), dma((STEPS, 2, chips)), dma((STEPS, 2, chips)),
        ],
        compiler_params=pltpu.CompilerParams(
            collective_id=0, has_side_effects=True, vmem_limit_bytes=56 * 1024 * 1024
        ),
    )(conc, mask, layer, stiff, prod, diff_tab, upt_tab)


def solution(mesh):
    cells = P("ax", "xs", None)
    return jax.shard_map(
        functools.partial(on_device, mesh.shape["ax"], mesh.shape["xs"]),
        mesh=mesh, in_specs=(cells,) * 5 + (P(), P()), out_specs=cells, check_vma=False,
    )
```
